32 devices in a mesh: tile: 16 (over z, y, x), dp: 2 (over core).
Axes of the slice: x: 2, y: 2, z: 4, core: 2. Of those that a mesh axis runs over, the one named last changes fastest.
Arguments:
- observations: bfloat16 [32768, 256], P(('dp', 'tile')), parts along dimension 0, may hold values from -6 to 6
- instrument: int32 [32768], P(('dp', 'tile')), parts along dimension 0, may hold values from 0 to 31
- route: int32 [32768, 1], P(('dp', 'tile')), parts along dimension 0, may hold values from 0 to 15; in each aligned block of 1024 rows (0 to 1023, 1024 to 2047, ...) at most 128 rows name the same one
- cell_index: int32 [32768], P(('dp', 'tile')), parts along dimension 0, may hold values from 0 to 255
- latent: bfloat16 [8192, 512], P(('dp', 'tile')), parts along dimension 0, may hold values from -6 to 6
- inst_table: bfloat16 [32, 256], replicated, may hold values from -4 to 4
- w_obs_kv: bfloat16 [256, 1024], replicated, may hold values from -0.375 to 0.375
- w_cross_q: bfloat16 [512, 512], replicated, may hold values from -0.25 to 0.25
- w_cross_out: bfloat16 [512, 512], replicated, may hold values from -0.25 to 0.25
- w_win_qkv: bfloat16 [512, 1536], replicated, may hold values from -0.25 to 0.25
- w_win_out: bfloat16 [512, 512], replicated, may hold values from -0.25 to 0.25
- w_up: bfloat16 [512, 2048], replicated, may hold values from -0.25 to 0.25
- w_down: bfloat16 [2048, 512], replicated, may hold values from -0.125 to 0.125
- cotangent: bfloat16 [8192, 512], P(('dp', 'tile')), parts along dimension 0, may hold values from -6 to 6
Outputs:
- latent_out: bfloat16 [8192, 512], P(('dp', 'tile')), parts along dimension 0
- grad_down: float32 [4096, 512], P('dp'), parts along dimension 0
The draws below stay inside these ranges and needn't reach their ends.
There are 2 independent parts, one for each index of `dp`. The reference program is written for one: setup_inputs(seed, part) draws one part's arguments, and reference() takes and returns one part's arrays. A program takes and returns all parts, laid end to end along the dimension named above; an argument that names none is the same for every part. Nothing has to cross between parts.
Inputs may be any that keep to these rules, and one draw needn't show every extreme that they name: `route`: among the 1024 observations of one index of tile, at most 128 name the same tile, and this bound is met; every tile is named by some observation.
All inputs are finite; a program needn't handle non-finite values.
Results may differ from the reference program's by a relative error of at most 0.0072.
Values may be sent and summed in bfloat16 or wider, within the bound.
No kernel may reach another device: no remote copies, remote signals or barrier semaphores. Data moves between devices by JAX's collectives and lax.ppermute only.
A program may use at most 128 MiB of HBM per device.

```python
import math
import jax
import jax.numpy as jnp
import numpy as np
from jax import lax

C = 256
D = 512
H = 8
FF = 2048
NINST = 32
OBS_DEV = 1024
LAT = 256
HW = 128
CAP = 128
TOTAL_OBS = 16384
CELLS = 4096
N_TILE = 16


def with_ends(entries, key, least, top_value):
    longest = entries.shape.index(max(entries.shape))
    spots = []
    for shift in (0, 1):
        where = [jax.random.randint(jax.random.fold_in(key, axis), (), 0, length) for axis, length in enumerate(entries.shape)]
        where[longest] = (where[longest] + shift) % entries.shape[longest]
        spots.append(tuple(where))
    return entries.at[spots[0]].set(least).at[spots[1]].set(top_value)


def block_scale(key, shape, cuts, smallest, top_value):
    def one(position, parts):
        heights = jax.random.uniform(jax.random.fold_in(jax.random.fold_in(key, 6), position), (parts,), jnp.float32, smallest / len(cuts), top_value / len(cuts))
        return jnp.repeat(jnp.exp(heights), shape[position] // parts).reshape((-1,) + (1,) * (len(shape) - position - 1))

    level = one(*cuts[0])
    for cut in cuts[1:]:
        level = level * one(*cut)
    return level


def routed_block(key, own, number, rows, amount, top, most, slope):
    ranking = jax.random.permutation(key, amount)
    heavy_load, usual = load_shares(amount, rows * top, most, slope, True), load_shares(amount, rows * top, most, slope, False)
    places = jnp.arange(amount)

    def named(sizes, turn):
        used = int((sizes > 0).sum())
        fixed = max(1, used // 4)
        moved = fixed + (places - fixed + turn * (used - fixed)) % max(1, amount - fixed)
        return jnp.zeros((amount,), jnp.int32).at[ranking[jnp.where(places < fixed, places, moved)]].set(jnp.asarray(sizes, jnp.int32))

    sizes = jnp.where(number % 4 == 0, named(heavy_load, number // 4), named(usual, number - number // 4 - 1))
    mixed = jax.random.permutation(jax.random.fold_in(own, 3), amount)
    giver, taker = mixed[0:amount // 2 * 2:2], mixed[1:amount // 2 * 2:2]
    room = jnp.minimum(sizes[giver] - 1, most - sizes[taker]) // 2
    room = jnp.where((giver == ranking[0]) | (taker == ranking[0]) | (sizes[taker] == 0), 0, jnp.maximum(room, 0))
    moved = jax.random.randint(jax.random.fold_in(own, 4), (amount // 2,), 0, 1 << 20) % (room + 1)
    sizes = sizes.at[giver].add(-moved).at[taker].add(moved)
    labels = jnp.searchsorted(jnp.cumsum(sizes), jnp.arange(rows * top), side="right").astype(jnp.int32)
    listing = labels.reshape(top, rows).T
    listing = listing[jax.random.permutation(jax.random.fold_in(own, 1), rows)]
    turn = jax.random.randint(jax.random.fold_in(own, 2), (rows, 1), 0, top)
    return jnp.take_along_axis(listing, (jnp.arange(top)[None, :] + turn) % top, axis=1)


def load_shares(count, total, limit, lean, full):
    loads = [(1 << 20) // math.isqrt(rank ** lean) + 1 for rank in range(1, count + 1)]
    largest = limit if full else min(limit, max(-(-total // count), total * loads[0] // sum(loads)))
    least = 1 if total - largest >= count - 1 else 0
    holding, spare = [largest] + [least] * (count - 1), total - largest - least * (count - 1)
    while spare > 0:
        free = [i for i in range(1, count) if holding[i] < largest] or [i for i in range(1, count) if holding[i] < limit]
        pool, remaining = sum([loads[i] for i in free]), spare
        for i in free:
            more = min(limit - holding[i], max(1, remaining * loads[i] // pool), spare)
            holding[i] = holding[i] + more
            spare = spare - more
    return np.array(holding)


def scatter_about(rng, extent, spread, most, split=(), kind=jnp.bfloat16):
    level = block_scale(rng, extent, split, -0.22, 0.18) if split else 1.0
    values = jax.random.normal(rng, extent, jnp.float32) * spread * level
    return jnp.minimum(jnp.maximum(values, -most), most).astype(kind)


def setup_inputs(seed: int = 0, part: int = 0) -> dict:
    arg_keys = jax.random.split(jax.random.key(seed), 15)
    part_splits = jax.random.split(jax.random.fold_in(arg_keys[14], part), 15)
    observations = scatter_about(part_splits[0], (TOTAL_OBS, C), 1.0, 6.0, ((0, 16),))
    instrument = with_ends(jax.random.randint(part_splits[1], (TOTAL_OBS,), 0, NINST), jax.random.fold_in(part_splits[1], 1), 0, NINST - 1).astype(jnp.int32)
    route_keys = jax.random.split(jax.random.fold_in(part_splits[2], 1), TOTAL_OBS // OBS_DEV)
    route_turns = jax.random.permutation(jax.random.fold_in(part_splits[2], 3), TOTAL_OBS // OBS_DEV)
    route = jax.vmap(lambda own, number: routed_block(jax.random.fold_in(part_splits[2], 2), own, number, OBS_DEV, N_TILE, 1, CAP, 2))(route_keys, route_turns).reshape((TOTAL_OBS, 1))
    cell_index = with_ends(jax.random.randint(part_splits[3], (TOTAL_OBS,), 0, LAT), jax.random.fold_in(part_splits[3], 1), 0, LAT - 1).astype(jnp.int32)
    latent = scatter_about(part_splits[4], (CELLS, D), 1.0, 6.0, ((0, 16),))
    inst_table = scatter_about(arg_keys[5], (NINST, C), 0.7, 4.0)
    w_obs_kv = scatter_about(arg_keys[6], (C, 2 * D), C ** -0.5, 0.375)
    w_cross_q = scatter_about(arg_keys[7], (D, D), D ** -0.5, 0.25)
    w_cross_out = scatter_about(arg_keys[8], (D, D), D ** -0.5, 0.25)
    w_win_qkv = scatter_about(arg_keys[9], (D, 3 * D), D ** -0.5, 0.25)
    w_win_out = scatter_about(arg_keys[10], (D, D), D ** -0.5, 0.25)
    w_up = scatter_about(arg_keys[11], (D, FF), D ** -0.5, 0.25)
    w_down = scatter_about(arg_keys[12], (FF, D), FF ** -0.5, 0.125)
    cotangent = scatter_about(part_splits[13], (CELLS, D), 1.0, 6.0, ((0, 16),))
    return dict(observations=observations, instrument=instrument, route=route, cell_index=cell_index, latent=latent, inst_table=inst_table, w_obs_kv=w_obs_kv, w_cross_q=w_cross_q, w_cross_out=w_cross_out, w_win_qkv=w_win_qkv, w_win_out=w_win_out, w_up=w_up, w_down=w_down, cotangent=cotangent)


def rms_norm(values):
    return values * lax.rsqrt(lax.optimization_barrier(jnp.mean(values * values, axis=-1, keepdims=True)) + 1e-06)

def attend(query, keys, values, bias, allowed):
    head_size = query.shape[1] // H
    query_heads = query.astype(jnp.float32).reshape(query.shape[0], H, head_size)
    key_heads = keys.astype(jnp.float32).reshape(keys.shape[0], H, head_size)
    value_heads = values.astype(jnp.float32).reshape(values.shape[0], H, head_size)
    scores = jnp.einsum('lhd,rhd->hlr', query_heads, key_heads) * head_size ** (-0.5) + bias[None]
    scores = jnp.where(allowed[None], scores, -1e+30)
    row_peak = lax.optimization_barrier(jnp.max(scores, axis=2, keepdims=True))
    expo = jnp.exp(scores - row_peak)
    row_total = lax.optimization_barrier(jnp.sum(expo, axis=2, keepdims=True))
    weights = (expo / row_total).astype(jnp.bfloat16).astype(jnp.float32)
    mixed = jnp.einsum('hlr,rhd->lhd', weights, value_heads)
    return mixed.astype(jnp.bfloat16).reshape(query.shape[0], query.shape[1])

def reference(observations, instrument, route, cell_index, latent, inst_table, w_obs_kv, w_cross_q, w_cross_out, w_win_qkv, w_win_out, w_up, w_down, cotangent):
    embedded = (observations.astype(jnp.float32) + inst_table.astype(jnp.float32)[instrument]).astype(jnp.bfloat16)
    target = route[:, 0]
    order = jnp.argsort(target, stable=True)
    counts = jax.ops.segment_sum(jnp.ones_like(target), target, num_segments=N_TILE).astype(jnp.int32)
    starts = (jnp.cumsum(counts) - counts).astype(jnp.int32)
    span = N_TILE * CAP
    sorted_obs = jnp.concatenate([embedded[order], jnp.zeros((span, C), jnp.bfloat16)], 0)
    sorted_cell = jnp.concatenate([cell_index[order], jnp.zeros((span,), jnp.int32)], 0)
    latent_f = latent.astype(jnp.float32)
    query_all = jnp.dot(rms_norm(latent_f).astype(jnp.bfloat16), w_cross_q, preferred_element_type=jnp.float32).astype(jnp.bfloat16)
    positions = jnp.arange(LAT).astype(jnp.float32)

    def cross_tile(tile):
        begin = starts[tile]
        rows = lax.dynamic_slice_in_dim(sorted_obs, begin, span, 0)
        cells_here = lax.dynamic_slice_in_dim(sorted_cell, begin, span, 0).astype(jnp.float32)
        present = jnp.arange(span).astype(jnp.int32) < counts[tile]
        obs_kv = jnp.dot(rows, w_obs_kv, preferred_element_type=jnp.float32).astype(jnp.bfloat16)
        query = lax.dynamic_slice_in_dim(query_all, (tile * LAT).astype(jnp.int32), LAT, 0)
        bias = -4.0 * jnp.abs(positions[:, None] - cells_here[None, :]) / LAT
        allowed = jnp.broadcast_to(present[None, :], (LAT, span))
        return attend(query, obs_kv[:, :D], obs_kv[:, D:], bias, allowed)
    cross = lax.map(cross_tile, jnp.arange(N_TILE).astype(jnp.int32)).reshape(CELLS, D)
    stream = latent_f + jnp.dot(cross, w_cross_out, preferred_element_type=jnp.float32)
    projected = jnp.dot(rms_norm(stream).astype(jnp.bfloat16), w_win_qkv, preferred_element_type=jnp.float32).astype(jnp.bfloat16)
    offsets = jnp.arange(LAT + 2 * HW)[None, :] - jnp.arange(LAT)[:, None]
    window_mask = (offsets >= 0) & (offsets <= 2 * HW)
    zero_bias = jnp.zeros((LAT, LAT + 2 * HW), jnp.float32)

    def window_tile(tile):
        index = ((tile * LAT - HW + jnp.arange(LAT + 2 * HW).astype(jnp.int32)) % CELLS).astype(jnp.int32)
        keys_here = jnp.take(projected[:, D:2 * D], index, axis=0)
        values_here = jnp.take(projected[:, 2 * D:], index, axis=0)
        query = lax.dynamic_slice_in_dim(projected[:, :D], (tile * LAT).astype(jnp.int32), LAT, 0)
        return attend(query, keys_here, values_here, zero_bias, window_mask)
    windowed = lax.map(window_tile, jnp.arange(N_TILE).astype(jnp.int32)).reshape(CELLS, D)
    stream = stream + jnp.dot(windowed, w_win_out, preferred_element_type=jnp.float32)
    hidden = jax.nn.gelu(jnp.dot(rms_norm(stream).astype(jnp.bfloat16), w_up, preferred_element_type=jnp.float32)).astype(jnp.bfloat16)
    latent_out = (stream + jnp.dot(hidden, w_down, preferred_element_type=jnp.float32)).astype(jnp.bfloat16)
    gradient = jnp.dot(hidden.T, cotangent, preferred_element_type=jnp.float32)
    factor = jnp.minimum(1.0, 0.5 / jnp.sqrt(jnp.mean(gradient * gradient) + 1e-06))
    return (latent_out, gradient * factor)
```

```python
import functools
import jax
import jax.numpy as jnp
from jax import lax
from jax.experimental import pallas as pl
from jax.experimental.pallas import tpu as pltpu
from jax.sharding import PartitionSpec as P

H = 8
LANES = 128
BF = jnp.bfloat16
F32 = jnp.float32
VMEM_LIMIT = 48 * 1024 * 1024


def dot(a, b, dims=((1,), (0,))):
    return lax.dot_general(a, b, (dims, ((), ())), preferred_element_type=F32)


def rms_norm(values):
    return values * lax.rsqrt(jnp.mean(values * values, axis=-1, keepdims=True) + 1e-06)


def iota(shape, dim):
    return lax.broadcasted_iota(jnp.int32, shape, dim)


def call(kernel, out_shape, flops, moved, scratch=(), in_specs=None, transcendentals=0):
    kwargs = {} if in_specs is None else {"in_specs": in_specs}
    return pl.pallas_call(
        kernel,
        out_shape=out_shape,
        scratch_shapes=scratch,
        compiler_params=pltpu.CompilerParams(vmem_limit_bytes=VMEM_LIMIT),
        cost_estimate=pl.CostEstimate(
            flops=flops, bytes_accessed=moved, transcendentals=transcendentals
        ),
        **kwargs,
    )


def pack_kernel(obs, inst, route, cell, table, out, *, tiles, cap):
    rows, channels = obs.shape
    kinds = (iota((table.shape[0], rows), 0) == inst[...]).astype(F32).astype(BF)
    embedded = (obs[...].astype(F32) + dot(kinds, table[...], ((0,), (0,)))).astype(BF)
    chosen = (iota((tiles, rows), 0) == route[...]).astype(F32)
    pieces = rows // LANES
    stacked = jnp.concatenate(
        [chosen[:, i * LANES : (i + 1) * LANES] for i in range(pieces)], axis=0
    )
    upto = (iota((LANES, LANES), 0) <= iota((LANES, LANES), 1)).astype(F32).astype(BF)
    counted = dot(stacked.astype(BF), upto)
    base = jnp.zeros((tiles, 1), F32)
    parts = []
    for i in range(pieces):
        part = counted[i * tiles : (i + 1) * tiles]
        parts.append(part + base)
        base = base + part[:, LANES - 1 :]
    place = jnp.concatenate(parts, axis=1)
    rank = (jnp.sum(chosen * place, axis=0, keepdims=True) - 1.0).astype(jnp.int32)
    mark = chosen * (cell[...] + 1).astype(F32)
    at_rank = (iota((cap, rows), 0) == rank).astype(F32).astype(BF)
    marks = dot(mark.astype(BF), at_rank, ((1,), (1,))).astype(BF)
    slot = route[...] * cap + rank
    step = min(256, tiles * cap)
    for first in range(0, tiles * cap, step):
        pick = (iota((step, rows), 0) + first == slot).astype(F32).astype(BF)
        moved = dot(pick, embedded).astype(BF)
        for i in range(step // cap):
            t = first // cap + i
            for c in range(channels // LANES):
                out[t, c * cap : (c + 1) * cap, :] = moved[
                    i * cap : (i + 1) * cap, c * LANES : (c + 1) * LANES
                ]
    tail = out.shape[1] - (channels // LANES) * cap
    if cap < LANES:
        marks = jnp.concatenate([marks, jnp.zeros((tiles, LANES - cap), BF)], axis=1)
    for t in range(tiles):
        out[t, (channels // LANES) * cap :, :] = jnp.broadcast_to(
            marks[t : t + 1, :].astype(F32), (tail, LANES)
        ).astype(BF)


def heads_pair(query, keys, values, add):
    low = iota(query.shape, 1) < query.shape[1] // 2
    zero = jnp.zeros_like(query)
    with_ones = jnp.concatenate([values, jnp.ones_like(values)], axis=1)
    results = []
    for q in (jnp.where(low, query, zero), jnp.where(low, zero, query)):
        scores = dot(q, keys, ((1,), (1,))) + add
        expo = jnp.exp(scores - jnp.max(scores, axis=1, keepdims=True)).astype(BF)
        mixed = dot(expo, with_ones)
        results.append(mixed[:, : query.shape[1]] / mixed[:, query.shape[1] :])
    return jnp.where(low, results[0], results[1]).astype(BF)


def cross_kernel(
    arrived, marks, latent, w_kv, w_q, w_out, stream_out, top, bottom, x, kv, q, add, cross, *, cap
):
    tiles = arrived.shape[0]
    cells, width = latent.shape
    for s in range(tiles):
        for c in range(x.shape[1] // LANES):
            x[s * cap : (s + 1) * cap, c * LANES : (c + 1) * LANES] = arrived[
                s, c * cap : (c + 1) * cap, :
            ]
    kv[...] = dot(x[...], w_kv[...]).astype(BF)
    latent_f = latent[...].astype(F32)
    scale = (width // H) ** -0.5
    q[...] = (dot(rms_norm(latent_f).astype(BF), w_q[...]).astype(BF).astype(F32) * scale).astype(
        BF
    )
    mark = marks[...]
    positions = iota((cells, 1), 0).astype(F32)
    add[...] = jnp.where(mark > 0.5, -4.0 * jnp.abs(positions - (mark - 1.0)) / cells, -1e30)

    def pair(p, carry):
        at = pl.multiple_of(p * LANES, LANES)
        cross[:, pl.ds(at, LANES)] = heads_pair(
            q[:, pl.ds(at, LANES)],
            kv[:, pl.ds(at, LANES)],
            kv[:, pl.ds(pl.multiple_of(width + p * LANES, LANES), LANES)],
            add[...],
        )
        return carry

    lax.fori_loop(0, width // LANES, pair, 0)
    stream = latent_f + dot(cross[...], w_out[...])
    stream_out[...] = stream
    normed = rms_norm(stream).astype(BF)
    top[...] = normed[: cells // 2]
    bottom[...] = normed[cells // 2 :]


def window_kernel(
    stream_in,
    before,
    top,
    bottom,
    after,
    w_qkv,
    w_out,
    w_up,
    stream_out,
    hidden,
    sliced,
    around,
    kv,
    q,
    add,
    mixed,
):
    cells, width = stream_in.shape
    reach = cells // 2
    for i, part in enumerate((before, top, bottom, after)):
        around[i * reach : (i + 1) * reach, :] = part[...]
    kv[...] = dot(around[...], w_qkv[:, width:]).astype(BF)
    scale = (width // H) ** -0.5
    own = around[reach : reach + cells, :]
    q[...] = (dot(own, w_qkv[:, :width]).astype(BF).astype(F32) * scale).astype(BF)
    offsets = iota(add.shape, 1) - iota(add.shape, 0)
    add[...] = jnp.where((offsets >= 0) & (offsets <= 2 * reach), 0.0, -1e30)

    def pair(p, carry):
        at = pl.multiple_of(p * LANES, LANES)
        mixed[:, pl.ds(at, LANES)] = heads_pair(
            q[:, pl.ds(at, LANES)],
            kv[:, pl.ds(at, LANES)],
            kv[:, pl.ds(pl.multiple_of(width + p * LANES, LANES), LANES)],
            add[...],
        )
        return carry

    lax.fori_loop(0, width // LANES, pair, 0)
    stream = stream_in[...] + dot(mixed[...], w_out[...])
    stream_out[...] = stream
    normed = rms_norm(stream).astype(BF)
    tiles, _, part = sliced.shape
    step = 512
    for first in range(0, hidden.shape[1], step):
        block = jax.nn.gelu(dot(normed, w_up[:, first : first + step])).astype(BF)
        hidden[:, first : first + step] = block
        if part == LANES:
            for i in range(step // LANES):
                sliced[first // LANES + i] = block[:, i * LANES : (i + 1) * LANES]


def down_kernel(stream, hidden, w_down, out):
    out[...] = (stream[...] + dot(hidden[...], w_down[...])).astype(BF)


def gradient_kernel(hidden, cotangent, out):
    out[...] = dot(hidden[...], cotangent[...], ((0,), (0,))).astype(BF)


def clip_kernel(me, *refs, order):
    pieces, out = refs[:-1], refs[-1]
    total = jnp.zeros((1, 1), F32)
    for piece in pieces:
        for i in range(piece.shape[0]):
            v = piece[i].astype(F32)
            total = total + jnp.sum(jnp.sum(v * v, axis=0, keepdims=True), axis=1, keepdims=True)
    factor = jnp.minimum(1.0, 0.5 / jnp.sqrt(total / (out.shape[0] * out.shape[1]) + 1e-06))
    for piece, steps in zip(pieces, order, strict=True):
        rows = piece.shape[1]
        for i, (flip, base, stride) in enumerate(steps):
            at = pl.multiple_of((me[0] ^ flip) * stride + base, rows)
            out[pl.ds(at, rows), :] = piece[i].astype(F32) * factor


def gathered(part, axis):
    count = lax.axis_size(axis)
    rows = part.shape[0]
    if count != 16 or rows % 32:
        whole = lax.all_gather(part, axis, axis=0)
        return [whole.reshape(1, count * rows, -1)], [[(0, 0, 0)]]

    def flipped(value, k):
        return lax.ppermute(value, axis, [(i, i ^ k) for i in range(count)])

    half = rows // 2
    column = (0, 4, 8, 12)
    stack = jnp.stack([part] + [flipped(part, k) for k in column[1:]], axis=0)
    first, second = stack[:, :half], stack[:, half:]
    first_1, second_1 = flipped(first, 1), flipped(second, 2)
    first = jnp.concatenate([first, first_1], axis=0)
    second = jnp.concatenate([second, second_1], axis=0)
    first_2, second_2 = flipped(first, 2), flipped(second, 1)
    order_a = [(k, 0, rows) for k in column] + [(k ^ 1, 0, rows) for k in column]
    order_b = [(k, half, rows) for k in column] + [(k ^ 2, half, rows) for k in column]
    return [first, first_2, second, second_2], [
        order_a,
        [(k ^ 2, b, s) for k, b, s in order_a],
        order_b,
        [(k ^ 1, b, s) for k, b, s in order_b],
    ]


def on_device(
    observations,
    instrument,
    route,
    cell_index,
    latent,
    inst_table,
    w_obs_kv,
    w_cross_q,
    w_cross_out,
    w_win_qkv,
    w_win_out,
    w_up,
    w_down,
    cotangent,
):
    tiles = lax.axis_size("tile")
    count, channels = observations.shape
    cells, width = latent.shape
    hidden_width = w_up.shape[1]
    cap = 2 * count // tiles
    keys = tiles * cap
    split = channels // LANES
    block_rows = split * cap + 8
    shape = jax.ShapeDtypeStruct

    payload = call(
        functools.partial(pack_kernel, tiles=tiles, cap=cap),
        shape((tiles, block_rows, LANES), BF),
        2 * keys * count * channels,
        2 * keys * channels + 2 * count * channels,
    )(
        observations,
        instrument.reshape(1, count),
        route.reshape(1, count),
        cell_index.reshape(1, count),
        inst_table,
    )
    arrived = lax.all_to_all(payload, "tile", split_axis=0, concat_axis=0, tiled=True)
    cot_all = lax.all_gather(cotangent, "tile", axis=0, tiled=True)
    marks = arrived[:, split * cap, :cap].reshape(1, keys).astype(F32)

    stream1, top, bottom = call(
        functools.partial(cross_kernel, cap=cap),
        (
            shape((cells, width), F32),
            shape((cells // 2, width), BF),
            shape((cells // 2, width), BF),
        ),
        4 * keys * channels * width + 4 * cells * keys * width,
        2 * keys * channels + 6 * width * width,
        scratch=[
            pltpu.VMEM((keys, channels), BF),
            pltpu.VMEM((keys, 2 * width), BF),
            pltpu.VMEM((cells, width), BF),
            pltpu.VMEM((cells, keys), F32),
            pltpu.VMEM((cells, width), BF),
        ],
        transcendentals=H * cells * keys,
    )(arrived, marks, latent, w_obs_kv, w_cross_q, w_cross_out)

    forward = [(i, (i + 1) % tiles) for i in range(tiles)]
    backward = [(b, a) for a, b in forward]
    before = lax.ppermute(bottom, "tile", forward)
    after = lax.ppermute(top, "tile", backward)

    part = hidden_width // tiles
    direct = part == LANES
    stream2, hidden, sliced = call(
        window_kernel,
        (
            shape((cells, width), F32),
            shape((cells, hidden_width), BF),
            shape((tiles, cells, part) if direct else (1, 16, LANES + 1), BF),
        ),
        2 * cells * width * (5 * width + hidden_width) + 8 * cells * cells * width,
        2 * width * (4 * width + hidden_width) + 4 * cells * hidden_width,
        scratch=[
            pltpu.VMEM((2 * cells, width), BF),
            pltpu.VMEM((2 * cells, 2 * width), BF),
            pltpu.VMEM((cells, width), BF),
            pltpu.VMEM((cells, 2 * cells), F32),
            pltpu.VMEM((cells, width), BF),
        ],
        transcendentals=2 * H * cells * cells + cells * hidden_width,
    )(stream1, before, top, bottom, after, w_win_qkv, w_win_out, w_up)
    if not direct:
        sliced = hidden.reshape(cells, tiles, part).transpose(1, 0, 2)
    swapped = lax.all_to_all(sliced, "tile", split_axis=0, concat_axis=0, tiled=True)
    latent_out = call(
        down_kernel,
        shape((cells, width), BF),
        2 * cells * width * hidden_width,
        2 * width * hidden_width + 2 * cells * hidden_width,
    )(stream2, hidden, w_down)
    gradient = call(
        gradient_kernel,
        shape((part, width), BF),
        2 * tiles * cells * part * width,
        2 * tiles * cells * (part + width),
    )(swapped.reshape(tiles * cells, part), cot_all)
    pieces, order = gathered(gradient, "tile")
    clipped = call(
        functools.partial(clip_kernel, order=order),
        shape((hidden_width, width), F32),
        4 * hidden_width * width,
        6 * hidden_width * width,
        in_specs=[pl.BlockSpec(memory_space=pltpu.SMEM)]
        + [pl.BlockSpec(memory_space=pltpu.VMEM)] * len(pieces),
    )(lax.axis_index("tile").reshape(1), *pieces)
    return (latent_out, clipped)


def solution(mesh):
    split = P(("dp", "tile"))
    rows = P(("dp", "tile"), None)
    return jax.shard_map(
        on_device,
        mesh=mesh,
        in_specs=(rows, split, rows, split, rows, P(), P(), P(), P(), P(), P(), P(), P(), rows),
        out_specs=(rows, P("dp", None)),
        check_vma=False,
    )
```

```python
import functools
import jax
import jax.numpy as jnp
from jax import lax
from jax.experimental import pallas as pl
from jax.experimental.pallas import tpu as pltpu
from jax.sharding import PartitionSpec as P

H = 8
LANES = 128
BF = jnp.bfloat16
F32 = jnp.float32
VMEM_LIMIT = 48 * 1024 * 1024
PLANE = 4


def dot(a, b, dims=((1,), (0,))):
    return lax.dot_general(a, b, (dims, ((), ())), preferred_element_type=F32)


def rms_norm(values):
    return values * lax.rsqrt(jnp.mean(values * values, axis=-1, keepdims=True) + 1e-06)


def iota(shape, dim):
    return lax.broadcasted_iota(jnp.int32, shape, dim)


def call(
    kernel, out_shape, flops, moved, scratch=(), in_specs=None, transcendentals=0, limit=VMEM_LIMIT
):
    kwargs = {} if in_specs is None else {"in_specs": in_specs}
    return pl.pallas_call(
        kernel,
        out_shape=out_shape,
        scratch_shapes=scratch,
        compiler_params=pltpu.CompilerParams(vmem_limit_bytes=limit),
        cost_estimate=pl.CostEstimate(
            flops=flops, bytes_accessed=moved, transcendentals=transcendentals
        ),
        **kwargs,
    )


def pack_kernel(*refs, tiles, cap):
    inputs, out, local, arrivals = refs[:5], refs[5], refs[6:11], refs[11]
    copies = [
        pltpu.make_async_copy(source, target, arrivals.at[i])
        for i, (source, target) in enumerate(zip(inputs, local, strict=True))
    ]
    for copy in copies:
        copy.start()
    for copy in copies:
        copy.wait()
    obs, inst, route, cell, table = local
    rows, channels = obs.shape
    kinds = (iota((table.shape[0], rows), 0) == inst[...]).astype(F32).astype(BF)
    embedded = (obs[...].astype(F32) + dot(kinds, table[...], ((0,), (0,)))).astype(BF)
    chosen = (iota((tiles, rows), 0) == route[...]).astype(F32)
    pieces = rows // LANES
    stacked = jnp.concatenate(
        [chosen[:, i * LANES : (i + 1) * LANES] for i in range(pieces)], axis=0
    )
    upto = (iota((LANES, LANES), 0) <= iota((LANES, LANES), 1)).astype(F32).astype(BF)
    counted = dot(stacked.astype(BF), upto)
    base = jnp.zeros((tiles, 1), F32)
    parts = []
    for i in range(pieces):
        part = counted[i * tiles : (i + 1) * tiles]
        parts.append(part + base)
        base = base + part[:, LANES - 1 :]
    place = jnp.concatenate(parts, axis=1)
    rank = (jnp.sum(chosen * place, axis=0, keepdims=True) - 1.0).astype(jnp.int32)
    mark = chosen * (cell[...] + 1).astype(F32)
    at_rank = (iota((cap, rows), 0) == rank).astype(F32).astype(BF)
    marks = dot(mark.astype(BF), at_rank, ((1,), (1,))).astype(BF)
    slot = route[...] * cap + rank
    step = min(256, tiles * cap)
    for first in range(0, tiles * cap, step):
        pick = (iota((step, rows), 0) + first == slot).astype(F32).astype(BF)
        moved = dot(pick, embedded).astype(BF)
        for i in range(step // cap):
            t = first // cap + i
            for c in range(channels // LANES):
                out[t, c * cap : (c + 1) * cap, :] = moved[
                    i * cap : (i + 1) * cap, c * LANES : (c + 1) * LANES
                ]
    tail = out.shape[1] - (channels // LANES) * cap
    if cap < LANES:
        marks = jnp.concatenate([marks, jnp.zeros((tiles, LANES - cap), BF)], axis=1)
    for t in range(tiles):
        out[t, (channels // LANES) * cap :, :] = jnp.broadcast_to(
            marks[t : t + 1, :].astype(F32), (tail, LANES)
        ).astype(BF)


def heads_pair(query, keys, values, add):
    low = iota(query.shape, 1) < query.shape[1] // 2
    zero = jnp.zeros_like(query)
    with_ones = jnp.concatenate([values, jnp.ones_like(values)], axis=1)
    results = []
    for q in (jnp.where(low, query, zero), jnp.where(low, zero, query)):
        scores = dot(q, keys, ((1,), (1,))) + add
        expo = jnp.exp(scores - jnp.max(scores, axis=1, keepdims=True)).astype(BF)
        mixed = dot(expo, with_ones)
        results.append(mixed[:, : query.shape[1]] / mixed[:, query.shape[1] :])
    return jnp.where(low, results[0], results[1]).astype(BF)


def cross_kernel(
    arrived, marks, latent, w_kv, w_q, w_out, stream_out, top, bottom, x, kv, q, add, cross, *, cap
):
    tiles = arrived.shape[0]
    cells, width = latent.shape
    for s in range(tiles):
        for c in range(x.shape[1] // LANES):
            x[s * cap : (s + 1) * cap, c * LANES : (c + 1) * LANES] = arrived[
                s, c * cap : (c + 1) * cap, :
            ]
    kv[...] = dot(x[...], w_kv[...]).astype(BF)
    latent_f = latent[...].astype(F32)
    scale = (width // H) ** -0.5
    q[...] = (dot(rms_norm(latent_f).astype(BF), w_q[...]).astype(BF).astype(F32) * scale).astype(
        BF
    )
    mark = marks[...]
    positions = iota((cells, 1), 0).astype(F32)
    add[...] = jnp.where(mark > 0.5, -4.0 * jnp.abs(positions - (mark - 1.0)) / cells, -1e30)

    def pair(p, carry):
        at = pl.multiple_of(p * LANES, LANES)
        cross[:, pl.ds(at, LANES)] = heads_pair(
            q[:, pl.ds(at, LANES)],
            kv[:, pl.ds(at, LANES)],
            kv[:, pl.ds(pl.multiple_of(width + p * LANES, LANES), LANES)],
            add[...],
        )
        return carry

    lax.fori_loop(0, width // LANES, pair, 0)
    stream = latent_f + dot(cross[...], w_out[...])
    stream_out[...] = stream
    normed = rms_norm(stream).astype(BF)
    top[...] = normed[: cells // 2]
    bottom[...] = normed[cells // 2 :]


def window_kernel(
    me,
    stream_in,
    before,
    top,
    bottom,
    after,
    w_qkv,
    w_out,
    w_up,
    stream_out,
    hidden,
    *refs,
):
    sliced, (around, kv, q, add, mixed) = refs[:-5], refs[-5:]
    cells, width = stream_in.shape
    reach = cells // 2
    for i, part in enumerate((before, top, bottom, after)):
        around[i * reach : (i + 1) * reach, :] = part[...]
    kv[...] = dot(around[...], w_qkv[:, width:]).astype(BF)
    scale = (width // H) ** -0.5
    own = around[reach : reach + cells, :]
    q[...] = (dot(own, w_qkv[:, :width]).astype(BF).astype(F32) * scale).astype(BF)
    offsets = iota(add.shape, 1) - iota(add.shape, 0)
    add[...] = jnp.where((offsets >= 0) & (offsets <= 2 * reach), 0.0, -1e30)

    def pair(p, carry):
        at = pl.multiple_of(p * LANES, LANES)
        mixed[:, pl.ds(at, LANES)] = heads_pair(
            q[:, pl.ds(at, LANES)],
            kv[:, pl.ds(at, LANES)],
            kv[:, pl.ds(pl.multiple_of(width + p * LANES, LANES), LANES)],
            add[...],
        )
        return carry

    lax.fori_loop(0, width // LANES, pair, 0)
    stream = stream_in[...] + dot(mixed[...], w_out[...])
    stream_out[...] = stream
    normed = rms_norm(stream).astype(BF)
    step = hidden.shape[1] // PLANE
    for j in range(PLANE):
        at = pl.multiple_of(((me[0] % PLANE) ^ j) * step, step)
        block = jax.nn.gelu(dot(normed, w_up[:, pl.ds(at, step)])).astype(BF)
        hidden[:, pl.ds(at, step)] = block
        if sliced:
            sliced[j][...] = block


def down_kernel(stream, hidden, w_down, out):
    out[...] = (stream[...] + dot(hidden[...], w_down[...])).astype(BF)


def gradient_kernel(hidden, cotangent, out):
    out[...] = dot(hidden[...], cotangent[...], ((0,), (0,))).astype(BF)


def plane_kernel(me, *refs):
    hidden, cotangent = refs[:PLANE], refs[PLANE : 2 * PLANE]
    own, others, total = refs[2 * PLANE], refs[2 * PLANE + 1 : -1], refs[-1]
    total[...] = sum(
        dot(h[...], c[...], ((0,), (0,))) for h, c in zip(hidden, cotangent, strict=True)
    )
    rows = own.shape[0]
    for i, out in enumerate((own, *others)):
        at = pl.multiple_of(((me[0] // PLANE) ^ i) * rows, rows)
        out[...] = total[pl.ds(at, rows), :].astype(out.dtype)


def clip_kernel(me, *refs, order):
    pieces, out = refs[:-1], refs[-1]
    total = jnp.zeros((1, 1), F32)
    for piece in pieces:
        for i in range(piece.shape[0]):
            v = piece[i].astype(F32)
            total = total + jnp.sum(jnp.sum(v * v, axis=0, keepdims=True), axis=1, keepdims=True)
    factor = jnp.minimum(1.0, 0.5 / jnp.sqrt(total / (out.shape[0] * out.shape[1]) + 1e-06))
    for piece, steps in zip(pieces, order, strict=True):
        rows = piece.shape[1]
        for i, step in enumerate(steps):
            at = 0
            if step is not None:
                flip, base, stride = step
                tile = me[0] ^ flip
                at = pl.multiple_of(
                    ((tile % PLANE) * PLANE + tile // PLANE) * stride + base, rows
                )
            out[pl.ds(at, rows), :] = piece[i].astype(F32) * factor


def flipped(value, k):
    return lax.ppermute(value, "tile", [(i, i ^ k) for i in range(PLANE * PLANE)])


def gathered(part):
    rows = part.shape[0]
    half = rows // 2
    column = tuple(PLANE * i for i in range(PLANE))
    stack = jnp.stack([part] + [flipped(part, k) for k in column[1:]], axis=0)
    first, second = stack[:, :half], stack[:, half:]
    first_1, second_1 = flipped(first, 1), flipped(second, 2)
    first = jnp.concatenate([first, first_1], axis=0)
    second = jnp.concatenate([second, second_1], axis=0)
    first_2, second_2 = flipped(first, 2), flipped(second, 1)
    order_a = [(k, 0, rows) for k in column] + [(k ^ 1, 0, rows) for k in column]
    order_b = [(k, half, rows) for k in column] + [(k ^ 2, half, rows) for k in column]
    return [first, first_2, second, second_2], [
        order_a,
        [(k ^ 2, b, s) for k, b, s in order_a],
        order_b,
        [(k ^ 1, b, s) for k, b, s in order_b],
    ]


def on_device(
    observations,
    instrument,
    route,
    cell_index,
    latent,
    inst_table,
    w_obs_kv,
    w_cross_q,
    w_cross_out,
    w_win_qkv,
    w_win_out,
    w_up,
    w_down,
    cotangent,
):
    tiles = lax.axis_size("tile")
    count, channels = observations.shape
    cells, width = latent.shape
    hidden_width = w_up.shape[1]
    cap = 2 * count // tiles
    keys = tiles * cap
    split = channels // LANES
    block_rows = split * cap + 8
    shape = jax.ShapeDtypeStruct

    payload = call(
        functools.partial(pack_kernel, tiles=tiles, cap=cap),
        shape((tiles, block_rows, LANES), BF),
        2 * keys * count * channels,
        2 * keys * channels + 2 * count * channels,
        in_specs=[pl.BlockSpec(memory_space=pltpu.HBM)] * 5,
        limit=62 * 1024 * 1024,
        scratch=[
            pltpu.VMEM((count, channels), BF),
            pltpu.VMEM((1, count), jnp.int32),
            pltpu.VMEM((1, count), jnp.int32),
            pltpu.VMEM((1, count), jnp.int32),
            pltpu.VMEM(inst_table.shape, BF),
            pltpu.SemaphoreType.DMA((5,)),
        ],
    )(
        observations,
        instrument.reshape(1, count),
        route.reshape(1, count),
        cell_index.reshape(1, count),
        inst_table,
    )
    arrived = lax.all_to_all(payload, "tile", split_axis=0, concat_axis=0, tiled=True)
    marks = arrived[:, split * cap, :cap].reshape(1, keys).astype(F32)

    stream1, top, bottom = call(
        functools.partial(cross_kernel, cap=cap),
        (
            shape((cells, width), F32),
            shape((cells // 2, width), BF),
            shape((cells // 2, width), BF),
        ),
        4 * keys * channels * width + 4 * cells * keys * width,
        2 * keys * channels + 6 * width * width,
        scratch=[
            pltpu.VMEM((keys, channels), BF),
            pltpu.VMEM((keys, 2 * width), BF),
            pltpu.VMEM((cells, width), BF),
            pltpu.VMEM((cells, keys), F32),
            pltpu.VMEM((cells, width), BF),
        ],
        transcendentals=H * cells * keys,
    )(arrived, marks, latent, w_obs_kv, w_cross_q, w_cross_out)

    forward = [(i, (i + 1) % tiles) for i in range(tiles)]
    backward = [(b, a) for a, b in forward]
    before = lax.ppermute(bottom, "tile", forward)
    after = lax.ppermute(top, "tile", backward)

    part = hidden_width // tiles
    me = lax.axis_index("tile").reshape(1)
    scalar, whole = pl.BlockSpec(memory_space=pltpu.SMEM), pl.BlockSpec(memory_space=pltpu.VMEM)
    fast = tiles == PLANE * PLANE
    quarter = hidden_width // PLANE
    stream2, hidden, *sliced = call(
        window_kernel,
        (
            shape((cells, width), F32),
            shape((cells, hidden_width), BF),
            *([shape((cells, quarter), BF)] * (PLANE if fast else 0)),
        ),
        2 * cells * width * (5 * width + hidden_width) + 8 * cells * cells * width,
        2 * width * (4 * width + hidden_width) + 4 * cells * hidden_width,
        scratch=[
            pltpu.VMEM((2 * cells, width), BF),
            pltpu.VMEM((2 * cells, 2 * width), BF),
            pltpu.VMEM((cells, width), BF),
            pltpu.VMEM((cells, 2 * cells), F32),
            pltpu.VMEM((cells, width), BF),
        ],
        in_specs=[scalar] + [whole] * 8,
        transcendentals=2 * H * cells * cells + cells * hidden_width,
    )(me, stream1, before, top, bottom, after, w_win_qkv, w_win_out, w_up)
    received = [flipped(sliced[j], j) for j in range(1, PLANE)] if fast else []
    latent_out = call(
        down_kernel,
        shape((cells, width), BF),
        2 * cells * width * hidden_width,
        2 * width * hidden_width + 2 * cells * hidden_width,
    )(stream2, hidden, w_down)
    if fast:
        late, _ = lax.optimization_barrier((cotangent, arrived))
        cotangents = [cotangent] + [flipped(late, j) for j in range(1, PLANE)]
        own, latent_out = lax.optimization_barrier((sliced[0], latent_out))
        mine, *others = call(
            plane_kernel,
            (shape((part, width), F32), *([shape((part, width), BF)] * (PLANE - 1))),
            2 * PLANE * cells * quarter * width,
            2 * PLANE * cells * (quarter + width) + 2 * quarter * width,
            scratch=[pltpu.VMEM((quarter, width), F32)],
            in_specs=[scalar] + [whole] * (2 * PLANE),
        )(me, own, *received, *cotangents)
        for i, other in enumerate(others, 1):
            mine = mine + flipped(other, PLANE * i).astype(F32)
        pieces, order = gathered(mine.astype(BF))
    else:
        swapped = lax.all_to_all(
            hidden.reshape(cells, tiles, part).transpose(1, 0, 2),
            "tile",
            split_axis=0,
            concat_axis=0,
            tiled=True,
        )
        gradient = call(
            gradient_kernel,
            shape((part, width), BF),
            2 * tiles * cells * part * width,
            2 * tiles * cells * (part + width),
        )(
            swapped.reshape(tiles * cells, part),
            lax.all_gather(cotangent, "tile", axis=0, tiled=True),
        )
        pieces = [lax.all_gather(gradient, "tile", axis=0, tiled=True)[None]]
        order = [[None]]
    clipped = call(
        functools.partial(clip_kernel, order=order),
        shape((hidden_width, width), F32),
        4 * hidden_width * width,
        6 * hidden_width * width,
        in_specs=[scalar] + [whole] * len(pieces),
    )(me, *pieces)
    return (latent_out, clipped)


def solution(mesh):
    split = P(("dp", "tile"))
    rows = P(("dp", "tile"), None)
    return jax.shard_map(
        on_device,
        mesh=mesh,
        in_specs=(rows, split, rows, split, rows, P(), P(), P(), P(), P(), P(), P(), P(), rows),
        out_specs=(rows, P("dp", None)),
        check_vma=False,
    )
```

```python
import functools
import jax
import jax.numpy as jnp
from jax import lax
from jax.experimental import pallas as pl
from jax.experimental.pallas import tpu as pltpu
from jax.sharding import PartitionSpec as P

H = 8
LANES = 128
PLANE = 4
CHUNKS = 2
BF = jnp.bfloat16
F32 = jnp.float32
MIB = 1024 * 1024
NO_KEY = -1e30


def started(sources, targets, semaphores):
    copies = [
        pltpu.make_async_copy(source, target, semaphores.at[i])
        for i, (source, target) in enumerate(zip(sources, targets, strict=True))
    ]
    for copy in copies:
        copy.start()
    return copies


def dot(a, b, dims=((1,), (0,))):
    return lax.dot_general(a, b, (dims, ((), ())), preferred_element_type=F32)


def rms_norm(values):
    return values * lax.rsqrt(jnp.mean(values * values, axis=-1, keepdims=True) + 1e-06)


def iota(shape, dim):
    return lax.broadcasted_iota(jnp.int32, shape, dim)


SCALAR = pl.BlockSpec(memory_space=pltpu.SMEM)
WHOLE = pl.BlockSpec(memory_space=pltpu.VMEM)
FAR = pl.BlockSpec(memory_space=pltpu.HBM)


def call(kernel, out_shape, flops, moved, specs, scratch=(), transcendentals=0, *, limit):
    return pl.pallas_call(
        kernel,
        out_shape=out_shape,
        in_specs=specs,
        scratch_shapes=scratch,
        compiler_params=pltpu.CompilerParams(vmem_limit_bytes=limit * MIB),
        cost_estimate=pl.CostEstimate(
            flops=flops, bytes_accessed=moved, transcendentals=transcendentals
        ),
    )


def pack_kernel(*refs, tiles, cap):
    inputs, out, local, arrivals = refs[:5], refs[5], refs[6:11], refs[11]
    for copy in started(inputs, local, arrivals):
        copy.wait()
    obs, inst, route, cell, table = local
    rows, channels = obs.shape
    kinds = (iota((table.shape[0], rows), 0) == inst[...]).astype(F32).astype(BF)
    embedded = (obs[...].astype(F32) + dot(kinds, table[...], ((0,), (0,)))).astype(BF)
    chosen = (iota((tiles, rows), 0) == route[...]).astype(F32)
    pieces = rows // LANES
    stacked = jnp.concatenate(
        [chosen[:, i * LANES : (i + 1) * LANES] for i in range(pieces)], axis=0
    )
    upto = (iota((LANES, LANES), 0) <= iota((LANES, LANES), 1)).astype(F32).astype(BF)
    counted = dot(stacked.astype(BF), upto)
    base = jnp.zeros((tiles, 1), F32)
    parts = []
    for i in range(pieces):
        part = counted[i * tiles : (i + 1) * tiles]
        parts.append(part + base)
        base = base + part[:, LANES - 1 :]
    place = jnp.concatenate(parts, axis=1)
    rank = (jnp.sum(chosen * place, axis=0, keepdims=True) - 1.0).astype(jnp.int32)
    mark = chosen * (cell[...] + 1).astype(F32)
    at_rank = (iota((cap, rows), 0) == rank).astype(F32).astype(BF)
    marks = dot(mark.astype(BF), at_rank, ((1,), (1,)))
    slot = route[...] * cap + rank
    split = channels // LANES
    step = min(256, tiles * cap)
    if cap < LANES:
        marks = jnp.concatenate([marks, jnp.zeros((tiles, LANES - cap), F32)], axis=1)
    for first in range(0, tiles * cap, step):
        pick = (iota((step, rows), 0) + first == slot).astype(F32).astype(BF)
        moved = dot(pick, embedded).astype(BF)
        for i in range(step // cap):
            t = first // cap + i
            for c in range(split):
                out[t, c * cap : (c + 1) * cap, :] = moved[
                    i * cap : (i + 1) * cap, c * LANES : (c + 1) * LANES
                ]
            out[t, split * cap :, :] = jnp.broadcast_to(
                marks[t : t + 1, :], (out.shape[1] - split * cap, LANES)
            ).astype(BF)


def heads_pair(query, keys, values, add, earlier=None):
    low = iota(query.shape, 1) < query.shape[1] // 2
    zero = jnp.zeros_like(query)
    lanes = query.shape[1]
    with_ones = jnp.concatenate([values, jnp.ones_like(values)], axis=1)
    results = []
    for i, q in enumerate((jnp.where(low, query, zero), jnp.where(low, zero, query))):
        scores = dot(q, keys, ((1,), (1,))) + add
        peak = jnp.max(scores, axis=1, keepdims=True)
        if earlier is not None:
            at = i * (lanes // 2)
            peak = jnp.maximum(peak, earlier[0][:, at : at + 1])
        mixed = dot(jnp.exp(scores - peak).astype(BF), with_ones)
        results.append((jnp.broadcast_to(peak, query.shape), mixed[:, :lanes], mixed[:, lanes:]))
    peak, mixed, total = (jnp.where(low, a, b) for a, b in zip(*results, strict=True))
    if earlier is not None:
        weight = jnp.exp(earlier[0] - peak)
        mixed, total = mixed + weight * earlier[1], total + weight * earlier[2]
    return peak, mixed, total


def pairs(width, body):
    for at in range(0, width, LANES):
        body(slice(at, at + LANES), slice(width + at, width + at + LANES))


def project_query(normed, weights, width):
    scaled = dot(normed, weights).astype(BF).astype(F32) * (width // H) ** -0.5
    return scaled.astype(BF)


def unpack(blocks, x, cap):
    for s, block in enumerate(blocks):
        for c in range(x.shape[1] // LANES):
            x[s * cap : (s + 1) * cap, c * LANES : (c + 1) * LANES] = block[
                c * cap : (c + 1) * cap, :
            ]


def distance(mark, cells):
    positions = iota((cells, 1), 0).astype(F32)
    return jnp.where(mark > 0.5, -4.0 * jnp.abs(positions - (mark - 1.0)) / cells, NO_KEY)


def block_marks(blocks, row):
    return jnp.concatenate([block[row : row + 1, :] for block in blocks], axis=1).astype(F32)


def query_kernel(latent, w_q, q):
    normed = rms_norm(latent[...].astype(F32)).astype(BF)
    q[...] = project_query(normed, w_q[...], q.shape[1])


def cross_kernel(*refs, cap, inputs):
    (stream_out, top, bottom), refs, far = refs[inputs : inputs + 3], refs[inputs + 3 :], refs[:inputs]
    local, (x, kv, add, cross, arrivals) = refs[:inputs], refs[inputs:]
    copies = started(far, local, arrivals)
    arrived, w_kv, q, latent, w_out = local[:5]
    cells, width = latent.shape
    for i in (0, 1, *range(5, inputs)):
        copies[i].wait()
    blocks = [arrived.at[s] for s in range(arrived.shape[0])]
    unpack(blocks, x, cap)
    mark = local[5][...] if cap % LANES else block_marks(blocks, (x.shape[1] // LANES) * cap)
    kv[...] = dot(x[...], w_kv[...]).astype(BF)
    add[...] = distance(mark, cells)
    for i in (2, 3, 4):
        copies[i].wait()

    def body(at, beside):
        _, value, weight = heads_pair(q[:, at], kv[:, at], kv[:, beside], add[...])
        cross[:, at] = (value / weight).astype(BF)

    pairs(width, body)
    stream = latent[...].astype(F32) + dot(cross[...], w_out[...])
    stream_out[...] = stream
    normed = rms_norm(stream).astype(BF)
    top[...] = normed[: cells // 2]
    bottom[...] = normed[cells // 2 :]


def inner_kernel(top, bottom, w_qkv, q, peak, mixed, total, kv, own, add):
    cells, width = q.shape
    reach = cells // 2
    own[:reach, :] = top[...]
    own[reach:, :] = bottom[...]
    q[...] = project_query(own[...], w_qkv[:, :width], width)
    kv[...] = dot(own[...], w_qkv[:, width:]).astype(BF)
    offsets = iota(add.shape, 1) - iota(add.shape, 0)
    add[...] = jnp.where((offsets >= -reach) & (offsets <= reach), 0.0, NO_KEY)

    def body(at, beside):
        peak[:, at], mixed[:, at], total[:, at] = heads_pair(
            q[:, at], kv[:, at], kv[:, beside], add[...]
        )

    pairs(width, body)


def outer_kernel(
    stream_in, before, after, w_qkv, w_out, q, peak, mixed, total, stream_out, normed, kv, windowed
):
    cells, width = stream_in.shape
    reach = cells // 2
    kv[:reach, :] = dot(before[...], w_qkv[:, width:]).astype(BF)
    kv[reach:, :] = dot(after[...], w_qkv[:, width:]).astype(BF)
    offsets = iota((reach, reach), 1) - iota((reach, reach), 0)
    adds = [jnp.where(seen, 0.0, NO_KEY) for seen in (offsets >= 0, offsets <= 0)]

    def body(at, beside):
        for half in range(2):
            rows = slice(half * reach, (half + 1) * reach)
            _, value, weight = heads_pair(
                q[rows, at],
                kv[rows, at],
                kv[rows, beside],
                adds[half],
                (peak[rows, at], mixed[rows, at], total[rows, at]),
            )
            windowed[rows, at] = (value / weight).astype(BF)

    pairs(width, body)
    stream = stream_in[...] + dot(windowed[...], w_out[...])
    stream_out[...] = stream
    normed[...] = rms_norm(stream).astype(BF)


def up_kernel(me, normed, w_up, *outs, chunk):
    step = outs[0].shape[1]
    for j, out in enumerate(outs):
        first = ((me[0] % PLANE) ^ j) * (CHUNKS * step) + chunk * step
        at = pl.ds(pl.multiple_of(first, step), step)
        out[...] = jax.nn.gelu(dot(normed[...], w_up[:, at])).astype(BF)


def down_kernel(me, stream, w_down, *refs):
    hidden, out = refs[:-1], refs[-1]
    step = hidden[0].shape[1]
    total = stream[...]
    for i, block in enumerate(hidden):
        chunk, j = divmod(i, PLANE)
        first = ((me[0] % PLANE) ^ j) * (CHUNKS * step) + chunk * step
        total += dot(block[...], w_down[pl.ds(pl.multiple_of(first, step), step), :])
    out[...] = total.astype(BF)


def gradient_kernel(hidden, cotangent, out):
    out[...] = dot(hidden[...], cotangent[...], ((0,), (0,))).astype(BF)


def plane_kernel(me, *refs):
    hidden, cotangent, (own, other, total) = refs[:PLANE], refs[PLANE : 2 * PLANE], refs[2 * PLANE :]
    total[...] = sum(
        dot(h[...], c[...], ((0,), (0,))) for h, c in zip(hidden, cotangent, strict=True)
    )
    rows = own.shape[0]
    for i, out in enumerate((own, other)):
        at = pl.multiple_of(((me[0] // PLANE + i) % 2) * rows, rows)
        out[...] = total[pl.ds(at, rows), :].astype(out.dtype)


def clip_kernel(me, *refs, order, unit):
    pieces, out, sums = refs[:-2], refs[-2], refs[-1]
    quarter = out.shape[0] // PLANE
    where = []
    for piece, steps in zip(pieces, order, strict=True):
        for i, (flip, base, other) in enumerate(steps):
            tile = me[0] ^ flip
            half = (tile // PLANE + other) % 2
            where.append(((tile % PLANE) * quarter + base + half * unit, piece, i))
    for at, piece, i in where:
        v = piece[i].astype(F32)
        sums[pl.ds(at // unit, 1), :] = jnp.sum(v * v, axis=0, keepdims=True)
    total = jnp.sum(jnp.sum(sums[...], axis=0, keepdims=True), axis=1, keepdims=True)
    factor = jnp.minimum(1.0, 0.5 / jnp.sqrt(total / (out.shape[0] * out.shape[1]) + 1e-06))
    for at, piece, i in where:
        out[pl.ds(pl.multiple_of(at, unit), unit), :] = piece[i].astype(F32) * factor


def clip_whole_kernel(gradient, out):
    v = gradient[...].astype(F32)
    total = jnp.sum(jnp.sum(v * v, axis=0, keepdims=True), axis=1, keepdims=True)
    factor = jnp.minimum(1.0, 0.5 / jnp.sqrt(total / (out.shape[0] * out.shape[1]) + 1e-06))
    out[...] = v * factor


def flipped(value, k):
    return lax.ppermute(value, "tile", [(i, i ^ k) for i in range(PLANE * PLANE)])


def narrow(value):
    return value.astype(BF)


def reduced(own, other, base):
    own = narrow(own + flipped(other, PLANE).astype(F32))
    own = narrow(own.astype(F32) + flipped(own, 2 * PLANE).astype(F32))
    other = flipped(own, PLANE)
    own_x, other_y = flipped(own, 1), flipped(other, 2)
    own, other = jnp.stack([own, own_x]), jnp.stack([other, other_y])
    own_y, other_x = flipped(own, 2), flipped(other, 1)
    return [own, own_y, other, other_x], [
        [(0, base, 0), (1, base, 0)],
        [(2, base, 0), (3, base, 0)],
        [(0, base, 1), (2, base, 1)],
        [(1, base, 1), (3, base, 1)],
    ]


def on_device(
    observations,
    instrument,
    route,
    cell_index,
    latent,
    inst_table,
    w_obs_kv,
    w_cross_q,
    w_cross_out,
    w_win_qkv,
    w_win_out,
    w_up,
    w_down,
    cotangent,
):
    tiles = lax.axis_size("tile")
    count, channels = observations.shape
    cells, width = latent.shape
    hidden_width = w_up.shape[1]
    cap = 2 * count // tiles
    split = channels // LANES
    rows = split * cap + 8
    fast = tiles == PLANE * PLANE and cap == LANES
    me = lax.axis_index("tile").reshape(1) if fast else jnp.zeros((1,), jnp.int32)
    shape = jax.ShapeDtypeStruct
    stream_shape = shape((cells, width), F32)
    half_shape = shape((cells // 2, width), BF)
    query_shape = shape((cells, width), BF)

    packed = call(
        functools.partial(pack_kernel, tiles=tiles, cap=cap),
        shape((tiles, rows, LANES), BF),
        2 * tiles * cap * count * channels,
        2 * tiles * cap * channels + 2 * count * channels,
        [FAR] * 5,
        scratch=[
            pltpu.VMEM((count, channels), BF),
            pltpu.VMEM((1, count), jnp.int32),
            pltpu.VMEM((1, count), jnp.int32),
            pltpu.VMEM((1, count), jnp.int32),
            pltpu.VMEM(inst_table.shape, BF),
            pltpu.SemaphoreType.DMA((5,)),
        ],
        limit=62,
    )(
        observations,
        instrument.reshape(1, count),
        route.reshape(1, count),
        cell_index.reshape(1, count),
        inst_table,
    )

    keys = tiles * cap
    arrived = lax.all_to_all(packed, "tile", split_axis=0, concat_axis=0, tiled=True)
    if fast:
        cotangents = [flipped(cotangent, j) for j in range(1, PLANE)]
        arrived, *cotangents = lax.optimization_barrier((arrived, *cotangents))
        cotangents = [cotangent, *cotangents]
    query = call(
        query_kernel,
        query_shape,
        2 * cells * width * width,
        2 * width * width + 4 * cells * width,
        [WHOLE] * 2,
        limit=8,
    )(latent, w_cross_q)
    marks = [arrived[:, split * cap, :cap].reshape(1, keys).astype(F32)] if cap % LANES else []
    operands = (arrived, w_obs_kv, query, latent, w_cross_out, *marks)
    stream1, top, bottom = call(
        functools.partial(cross_kernel, cap=cap, inputs=len(operands)),
        (stream_shape, half_shape, half_shape),
        4 * keys * channels * width + 4 * cells * keys * width,
        2 * keys * channels + 6 * width * width,
        [FAR] * len(operands),
        scratch=[pltpu.VMEM(operand.shape, operand.dtype) for operand in operands]
        + [
            pltpu.VMEM((keys, channels), BF),
            pltpu.VMEM((keys, 2 * width), BF),
            pltpu.VMEM((cells, keys), F32),
            pltpu.VMEM((cells, width), BF),
            pltpu.SemaphoreType.DMA((len(operands),)),
        ],
        transcendentals=H * cells * keys,
        limit=62,
    )(*operands)

    forward = [(i, (i + 1) % tiles) for i in range(tiles)]
    backward = [(b, a) for a, b in forward]
    before = lax.ppermute(bottom, "tile", forward)
    after = lax.ppermute(top, "tile", backward)
    partial = call(
        inner_kernel,
        (query_shape, stream_shape, stream_shape, stream_shape),
        6 * cells * width * width + 4 * cells * cells * width,
        6 * width * width + 16 * cells * width,
        [WHOLE] * 3,
        scratch=[
            pltpu.VMEM((cells, 2 * width), BF),
            pltpu.VMEM((cells, width), BF),
            pltpu.VMEM((cells, cells), F32),
        ],
        transcendentals=H * cells * cells,
        limit=20,
    )(top, bottom, w_win_qkv)
    stream2, normed = call(
        outer_kernel,
        (stream_shape, query_shape),
        6 * cells * width * width + 2 * cells * cells * width,
        8 * width * width + 24 * cells * width,
        [WHOLE] * 9,
        scratch=[pltpu.VMEM((cells, 2 * width), BF), pltpu.VMEM((cells, width), BF)],
        transcendentals=H * cells * cells // 2,
        limit=20,
    )(stream1, before, after, w_win_qkv, w_win_out, *partial)

    step = hidden_width // (CHUNKS * PLANE)
    hidden = [
        call(
            functools.partial(up_kernel, chunk=c),
            [shape((cells, step), BF)] * PLANE,
            2 * cells * width * hidden_width // CHUNKS,
            2 * width * hidden_width // CHUNKS + 2 * cells * hidden_width // CHUNKS,
            [SCALAR, WHOLE, WHOLE],
            transcendentals=cells * hidden_width // CHUNKS,
            limit=12,
        )(me, normed, w_up)
        for c in range(CHUNKS)
    ]
    if fast:
        received = [[h[0]] + [flipped(h[j], j) for j in range(1, PLANE)] for h in hidden]
    latent_out = call(
        down_kernel,
        query_shape,
        2 * cells * width * hidden_width,
        2 * width * hidden_width + 2 * cells * hidden_width,
        [SCALAR] + [WHOLE] * (2 + CHUNKS * PLANE),
        limit=12,
    )(me, stream2, w_down, *[block for h in hidden for block in h])
    part = hidden_width // tiles
    if fast:
        received[0][0], latent_out = lax.optimization_barrier((received[0][0], latent_out))
        half = shape((step // 2, width), F32)
        pieces, order = [], []
        for c in range(CHUNKS):
            own, other = call(
                plane_kernel,
                (half, shape(half.shape, BF)),
                2 * PLANE * cells * step * width,
                2 * PLANE * cells * (step + width) + 2 * step * width,
                [SCALAR] + [WHOLE] * (2 * PLANE),
                scratch=[pltpu.VMEM((step, width), F32)],
                limit=12,
            )(me, *received[c], *cotangents)
            more, places = reduced(own, other, c * step)
            pieces, order = pieces + more, order + places
        clipped = call(
            functools.partial(clip_kernel, order=order, unit=step // 2),
            shape((hidden_width, width), F32),
            4 * hidden_width * width,
            6 * hidden_width * width,
            [SCALAR] + [WHOLE] * len(pieces),
            scratch=[pltpu.VMEM((2 * CHUNKS * PLANE, width), F32)],
            limit=24,
        )(me, *pieces)
    else:
        whole = jnp.concatenate([hidden[c][j] for j in range(PLANE) for c in range(CHUNKS)], 1)
        swapped = lax.all_to_all(
            whole.reshape(cells, tiles, part).transpose(1, 0, 2),
            "tile",
            split_axis=0,
            concat_axis=0,
            tiled=True,
        )
        gradient = call(
            gradient_kernel,
            shape((part, width), BF),
            2 * tiles * cells * part * width,
            2 * tiles * cells * (part + width),
            [WHOLE] * 2,
            limit=60,
        )(
            swapped.reshape(tiles * cells, part),
            lax.all_gather(cotangent, "tile", axis=0, tiled=True),
        )
        clipped = call(
            clip_whole_kernel,
            shape((hidden_width, width), F32),
            4 * hidden_width * width,
            6 * hidden_width * width,
            [WHOLE],
            limit=24,
        )(lax.all_gather(gradient, "tile", axis=0, tiled=True))
    return (latent_out, clipped)


def solution(mesh):
    split = P(("dp", "tile"))
    rows = P(("dp", "tile"), None)
    return jax.shard_map(
        on_device,
        mesh=mesh,
        in_specs=(rows, split, rows, split, rows, P(), P(), P(), P(), P(), P(), P(), P(), rows),
        out_specs=(rows, P("dp", None)),
        check_vma=False,
    )
```

```python
import functools
import jax
import jax.numpy as jnp
from jax import lax
from jax.experimental import pallas as pl
from jax.experimental.pallas import tpu as pltpu
from jax.sharding import PartitionSpec as P

H = 8
LANES = 128
PLANE = 4
CHUNKS = 2
DIRECT = (1,)
BF = jnp.bfloat16
F32 = jnp.float32
MIB = 1024 * 1024
NO_KEY = -1e30


def started(sources, targets, semaphores):
    copies = [
        pltpu.make_async_copy(source, target, semaphores.at[i])
        for i, (source, target) in enumerate(zip(sources, targets, strict=True))
    ]
    for copy in copies:
        copy.start()
    return copies


def dot(a, b, dims=((1,), (0,))):
    return lax.dot_general(a, b, (dims, ((), ())), preferred_element_type=F32)


def rms_norm(values):
    return values * lax.rsqrt(jnp.mean(values * values, axis=-1, keepdims=True) + 1e-06)


def iota(shape, dim):
    return lax.broadcasted_iota(jnp.int32, shape, dim)


SCALAR = pl.BlockSpec(memory_space=pltpu.SMEM)
WHOLE = pl.BlockSpec(memory_space=pltpu.VMEM)
FAR = pl.BlockSpec(memory_space=pltpu.HBM)


def call(kernel, out_shape, flops, moved, specs, scratch=(), transcendentals=0, out_spec=None, *, limit):
    kwargs = {} if out_spec is None else {"out_specs": out_spec}
    return pl.pallas_call(
        kernel,
        out_shape=out_shape,
        **kwargs,
        in_specs=specs,
        scratch_shapes=scratch,
        compiler_params=pltpu.CompilerParams(vmem_limit_bytes=limit * MIB),
        cost_estimate=pl.CostEstimate(
            flops=flops, bytes_accessed=moved, transcendentals=transcendentals
        ),
    )


def pack_kernel(*refs, tiles, cap):
    inputs, out, local, arrivals = refs[:5], refs[5], refs[6:11], refs[11]
    for copy in started(inputs, local, arrivals):
        copy.wait()
    obs, inst, route, cell, table = local
    rows, channels = obs.shape
    kinds = (iota((table.shape[0], rows), 0) == inst[...]).astype(F32).astype(BF)
    embedded = (obs[...].astype(F32) + dot(kinds, table[...], ((0,), (0,)))).astype(BF)
    chosen = (iota((tiles, rows), 0) == route[...]).astype(F32)
    pieces = rows // LANES
    stacked = jnp.concatenate(
        [chosen[:, i * LANES : (i + 1) * LANES] for i in range(pieces)], axis=0
    )
    upto = (iota((LANES, LANES), 0) <= iota((LANES, LANES), 1)).astype(F32).astype(BF)
    counted = dot(stacked.astype(BF), upto)
    base = jnp.zeros((tiles, 1), F32)
    parts = []
    for i in range(pieces):
        part = counted[i * tiles : (i + 1) * tiles]
        parts.append(part + base)
        base = base + part[:, LANES - 1 :]
    place = jnp.concatenate(parts, axis=1)
    rank = (jnp.sum(chosen * place, axis=0, keepdims=True) - 1.0).astype(jnp.int32)
    mark = chosen * (cell[...] + 1).astype(F32)
    at_rank = (iota((cap, rows), 0) == rank).astype(F32).astype(BF)
    marks = dot(mark.astype(BF), at_rank, ((1,), (1,)))
    slot = route[...] * cap + rank
    split = channels // LANES
    step = min(256, tiles * cap)
    if cap < LANES:
        marks = jnp.concatenate([marks, jnp.zeros((tiles, LANES - cap), F32)], axis=1)
    for first in range(0, tiles * cap, step):
        pick = (iota((step, rows), 0) + first == slot).astype(F32).astype(BF)
        moved = dot(pick, embedded).astype(BF)
        for i in range(step // cap):
            t = first // cap + i
            for c in range(split):
                out[t, c * cap : (c + 1) * cap, :] = moved[
                    i * cap : (i + 1) * cap, c * LANES : (c + 1) * LANES
                ]
            out[t, split * cap :, :] = jnp.broadcast_to(
                marks[t : t + 1, :], (out.shape[1] - split * cap, LANES)
            ).astype(BF)


def heads_pair(query, keys, values, add, earlier=None):
    low = iota(query.shape, 1) < query.shape[1] // 2
    zero = jnp.zeros_like(query)
    lanes = query.shape[1]
    with_ones = jnp.concatenate([values, jnp.ones_like(values)], axis=1)
    results = []
    for i, q in enumerate((jnp.where(low, query, zero), jnp.where(low, zero, query))):
        scores = dot(q, keys, ((1,), (1,))) + add
        peak = jnp.max(scores, axis=1, keepdims=True)
        if earlier is not None:
            at = i * (lanes // 2)
            peak = jnp.maximum(peak, earlier[0][:, at : at + 1])
        mixed = dot(jnp.exp(scores - peak).astype(BF), with_ones)
        results.append((jnp.broadcast_to(peak, query.shape), mixed[:, :lanes], mixed[:, lanes:]))
    peak, mixed, total = (jnp.where(low, a, b) for a, b in zip(*results, strict=True))
    if earlier is not None:
        weight = jnp.exp(earlier[0] - peak)
        mixed, total = mixed + weight * earlier[1], total + weight * earlier[2]
    return peak, mixed, total


def pairs(width, body):
    for at in range(0, width, LANES):
        body(slice(at, at + LANES), slice(width + at, width + at + LANES))


def project_query(normed, weights, width):
    scaled = dot(normed, weights).astype(BF).astype(F32) * (width // H) ** -0.5
    return scaled.astype(BF)


def unpack(blocks, x, cap):
    for s, block in enumerate(blocks):
        for c in range(x.shape[1] // LANES):
            x[s * cap : (s + 1) * cap, c * LANES : (c + 1) * LANES] = block[
                c * cap : (c + 1) * cap, :
            ]


def distance(mark, cells):
    positions = iota((cells, 1), 0).astype(F32)
    return jnp.where(mark > 0.5, -4.0 * jnp.abs(positions - (mark - 1.0)) / cells, NO_KEY)


def block_marks(blocks, row):
    return jnp.concatenate([block[row : row + 1, :] for block in blocks], axis=1).astype(F32)


def query_kernel(latent, w_q, q):
    normed = rms_norm(latent[...].astype(F32)).astype(BF)
    q[...] = project_query(normed, w_q[...], q.shape[1])


def cross_kernel(*refs, cap, inputs):
    (stream_out, top, bottom), refs, far = refs[inputs : inputs + 3], refs[inputs + 3 :], refs[:inputs]
    local, (x, kv, add, cross, arrivals) = refs[:inputs], refs[inputs:]
    copies = started(far, local, arrivals)
    arrived, w_kv, q, latent, w_out = local[:5]
    cells, width = latent.shape
    for i in (0, 1, *range(5, inputs)):
        copies[i].wait()
    blocks = [arrived.at[s] for s in range(arrived.shape[0])]
    unpack(blocks, x, cap)
    mark = local[5][...] if cap % LANES else block_marks(blocks, (x.shape[1] // LANES) * cap)
    kv[...] = dot(x[...], w_kv[...]).astype(BF)
    add[...] = distance(mark, cells)
    for i in (2, 3, 4):
        copies[i].wait()

    def body(at, beside):
        _, value, weight = heads_pair(q[:, at], kv[:, at], kv[:, beside], add[...])
        cross[:, at] = (value / weight).astype(BF)

    pairs(width, body)
    stream = latent[...].astype(F32) + dot(cross[...], w_out[...])
    stream_out[...] = stream
    normed = rms_norm(stream).astype(BF)
    top[...] = normed[: cells // 2]
    bottom[...] = normed[cells // 2 :]


def inner_kernel(top, bottom, w_qkv, q, peak, mixed, total, kv, own, add):
    cells, width = q.shape
    reach = cells // 2
    own[:reach, :] = top[...]
    own[reach:, :] = bottom[...]
    q[...] = project_query(own[...], w_qkv[:, :width], width)
    kv[...] = dot(own[...], w_qkv[:, width:]).astype(BF)
    offsets = iota(add.shape, 1) - iota(add.shape, 0)
    add[...] = jnp.where((offsets >= -reach) & (offsets <= reach), 0.0, NO_KEY)

    def body(at, beside):
        peak[:, at], mixed[:, at], total[:, at] = heads_pair(
            q[:, at], kv[:, at], kv[:, beside], add[...]
        )

    pairs(width, body)


def outer_kernel(
    stream_in, before, after, w_qkv, w_out, q, peak, mixed, total, stream_out, normed, kv, windowed
):
    cells, width = stream_in.shape
    reach = cells // 2
    kv[:reach, :] = dot(before[...], w_qkv[:, width:]).astype(BF)
    kv[reach:, :] = dot(after[...], w_qkv[:, width:]).astype(BF)
    offsets = iota((reach, reach), 1) - iota((reach, reach), 0)
    adds = [jnp.where(seen, 0.0, NO_KEY) for seen in (offsets >= 0, offsets <= 0)]

    def body(at, beside):
        for half in range(2):
            rows = slice(half * reach, (half + 1) * reach)
            _, value, weight = heads_pair(
                q[rows, at],
                kv[rows, at],
                kv[rows, beside],
                adds[half],
                (peak[rows, at], mixed[rows, at], total[rows, at]),
            )
            windowed[rows, at] = (value / weight).astype(BF)

    pairs(width, body)
    stream = stream_in[...] + dot(windowed[...], w_out[...])
    stream_out[...] = stream
    normed[...] = rms_norm(stream).astype(BF)


def up_kernel(me, normed, w_up, *outs, chunk):
    step = outs[0].shape[1]
    for j, out in enumerate(outs):
        first = ((me[0] % PLANE) ^ j) * (CHUNKS * step) + chunk * step
        at = pl.ds(pl.multiple_of(first, step), step)
        out[...] = jax.nn.gelu(dot(normed[...], w_up[:, at])).astype(BF)


def down_kernel(me, stream, w_down, *refs):
    hidden, out = refs[:-1], refs[-1]
    step = hidden[0].shape[1]
    total = stream[...]
    for i, block in enumerate(hidden):
        chunk, j = divmod(i, PLANE)
        first = ((me[0] % PLANE) ^ j) * (CHUNKS * step) + chunk * step
        total += dot(block[...], w_down[pl.ds(pl.multiple_of(first, step), step), :])
    out[...] = total.astype(BF)


def gradient_kernel(hidden, cotangent, out):
    out[...] = dot(hidden[...], cotangent[...], ((0,), (0,))).astype(BF)


def plane_kernel(me, *refs):
    hidden, cotangent, (own, other, total) = refs[:PLANE], refs[PLANE : 2 * PLANE], refs[2 * PLANE :]
    total[...] = sum(
        dot(h[...], c[...], ((0,), (0,))) for h, c in zip(hidden, cotangent, strict=True)
    )
    rows = own.shape[0]
    for i, out in enumerate((own, other)):
        at = pl.multiple_of(((me[0] // PLANE + i) % 2) * rows, rows)
        out[...] = total[pl.ds(at, rows), :].astype(out.dtype)


def clip_kernel(me, *refs, order, unit):
    pieces, (out, sums, scaled, sent) = refs[:-4], refs[-4:]
    quarter = out.shape[0] // PLANE
    where = []
    for piece, steps in zip(pieces, order, strict=True):
        for i, (flip, base, other) in enumerate(steps):
            tile = me[0] ^ flip
            half = (tile // PLANE + other) % 2
            where.append(((tile % PLANE) * quarter + base + half * unit, piece, i))
    for at, piece, i in where:
        v = piece[i].astype(F32)
        sums[pl.ds(at // unit, 1), :] = jnp.sum(v * v, axis=0, keepdims=True)
    total = jnp.sum(jnp.sum(sums[...], axis=0, keepdims=True), axis=1, keepdims=True)
    factor = jnp.minimum(1.0, 0.5 / jnp.sqrt(total / (out.shape[0] * out.shape[1]) + 1e-06))
    copies = []
    for n, (at, piece, i) in enumerate(where):
        scaled[n] = piece[i].astype(F32) * factor
        rows = pl.ds(pl.multiple_of(at, unit), unit)
        copies.append(pltpu.make_async_copy(scaled.at[n], out.at[rows, :], sent.at[n]))
        copies[-1].start()
    for copy in copies:
        copy.wait()


def clip_whole_kernel(gradient, out):
    v = gradient[...].astype(F32)
    total = jnp.sum(jnp.sum(v * v, axis=0, keepdims=True), axis=1, keepdims=True)
    factor = jnp.minimum(1.0, 0.5 / jnp.sqrt(total / (out.shape[0] * out.shape[1]) + 1e-06))
    out[...] = v * factor


def flipped(value, k):
    return lax.ppermute(value, "tile", [(i, i ^ k) for i in range(PLANE * PLANE)])


def narrow(value):
    return value.astype(BF)


def reduced(own, other, base, wait_for, direct):
    own = narrow(own + flipped(other, PLANE).astype(F32))
    across = flipped(own, 2 * PLANE)
    own = narrow(own.astype(F32) + across.astype(F32))
    if direct:
        owns = [own] + [flipped(own, j) for j in range(1, PLANE)]
        other = flipped(own, PLANE)
        others = [other] + [flipped(other, j) for j in range(1, PLANE)]
        return (
            [across],
            [half[None] for half in owns + others],
            [[(j, base, n)] for n in range(2) for j in range(PLANE)],
        )
    other = flipped(own, PLANE)
    own_x, other_y = flipped(own, 1), flipped(other, 2)
    own, other = jnp.stack([own, own_x]), jnp.stack([other, other_y])
    own_y, other_x = flipped(own, 2), flipped(other, 1)
    return (
        [across],
        [own, own_y, other, other_x],
        [
            [(0, base, 0), (1, base, 0)],
            [(2, base, 0), (3, base, 0)],
            [(0, base, 1), (2, base, 1)],
            [(1, base, 1), (3, base, 1)],
        ],
    )


def on_device(
    observations,
    instrument,
    route,
    cell_index,
    latent,
    inst_table,
    w_obs_kv,
    w_cross_q,
    w_cross_out,
    w_win_qkv,
    w_win_out,
    w_up,
    w_down,
    cotangent,
):
    tiles = lax.axis_size("tile")
    count, channels = observations.shape
    cells, width = latent.shape
    hidden_width = w_up.shape[1]
    cap = 2 * count // tiles
    split = channels // LANES
    rows = split * cap + 8
    fast = tiles == PLANE * PLANE and cap == LANES
    me = lax.axis_index("tile").reshape(1) if fast else jnp.zeros((1,), jnp.int32)
    shape = jax.ShapeDtypeStruct
    stream_shape = shape((cells, width), F32)
    half_shape = shape((cells // 2, width), BF)
    query_shape = shape((cells, width), BF)

    packed = call(
        functools.partial(pack_kernel, tiles=tiles, cap=cap),
        shape((tiles, rows, LANES), BF),
        2 * tiles * cap * count * channels,
        2 * tiles * cap * channels + 2 * count * channels,
        [FAR] * 5,
        scratch=[
            pltpu.VMEM((count, channels), BF),
            pltpu.VMEM((1, count), jnp.int32),
            pltpu.VMEM((1, count), jnp.int32),
            pltpu.VMEM((1, count), jnp.int32),
            pltpu.VMEM(inst_table.shape, BF),
            pltpu.SemaphoreType.DMA((5,)),
        ],
        limit=62,
    )(
        observations,
        instrument.reshape(1, count),
        route.reshape(1, count),
        cell_index.reshape(1, count),
        inst_table,
    )

    keys = tiles * cap
    arrived = lax.all_to_all(packed, "tile", split_axis=0, concat_axis=0, tiled=True)
    if fast:
        cotangents = [flipped(cotangent, j) for j in range(1, PLANE)]
        arrived, *cotangents = lax.optimization_barrier((arrived, *cotangents))
        cotangents = [cotangent, *cotangents]
    query = call(
        query_kernel,
        query_shape,
        2 * cells * width * width,
        2 * width * width + 4 * cells * width,
        [WHOLE] * 2,
        limit=8,
    )(latent, w_cross_q)
    marks = [arrived[:, split * cap, :cap].reshape(1, keys).astype(F32)] if cap % LANES else []
    operands = (arrived, w_obs_kv, query, latent, w_cross_out, *marks)
    stream1, top, bottom = call(
        functools.partial(cross_kernel, cap=cap, inputs=len(operands)),
        (stream_shape, half_shape, half_shape),
        4 * keys * channels * width + 4 * cells * keys * width,
        2 * keys * channels + 6 * width * width,
        [FAR] * len(operands),
        scratch=[pltpu.VMEM(operand.shape, operand.dtype) for operand in operands]
        + [
            pltpu.VMEM((keys, channels), BF),
            pltpu.VMEM((keys, 2 * width), BF),
            pltpu.VMEM((cells, keys), F32),
            pltpu.VMEM((cells, width), BF),
            pltpu.SemaphoreType.DMA((len(operands),)),
        ],
        transcendentals=H * cells * keys,
        limit=62,
    )(*operands)

    forward = [(i, (i + 1) % tiles) for i in range(tiles)]
    backward = [(b, a) for a, b in forward]
    before = lax.ppermute(bottom, "tile", forward)
    after = lax.ppermute(top, "tile", backward)
    partial = call(
        inner_kernel,
        (query_shape, stream_shape, stream_shape, stream_shape),
        6 * cells * width * width + 4 * cells * cells * width,
        6 * width * width + 16 * cells * width,
        [WHOLE] * 3,
        scratch=[
            pltpu.VMEM((cells, 2 * width), BF),
            pltpu.VMEM((cells, width), BF),
            pltpu.VMEM((cells, cells), F32),
        ],
        transcendentals=H * cells * cells,
        limit=20,
    )(top, bottom, w_win_qkv)
    stream2, normed = call(
        outer_kernel,
        (stream_shape, query_shape),
        6 * cells * width * width + 2 * cells * cells * width,
        8 * width * width + 24 * cells * width,
        [WHOLE] * 9,
        scratch=[pltpu.VMEM((cells, 2 * width), BF), pltpu.VMEM((cells, width), BF)],
        transcendentals=H * cells * cells // 2,
        limit=20,
    )(stream1, before, after, w_win_qkv, w_win_out, *partial)

    step = hidden_width // (CHUNKS * PLANE)
    hidden = [
        call(
            functools.partial(up_kernel, chunk=c),
            [shape((cells, step), BF)] * PLANE,
            2 * cells * width * hidden_width // CHUNKS,
            2 * width * hidden_width // CHUNKS + 2 * cells * hidden_width // CHUNKS,
            [SCALAR, WHOLE, WHOLE],
            transcendentals=cells * hidden_width // CHUNKS,
            limit=12,
        )(me, normed, w_up)
        for c in range(CHUNKS)
    ]
    if fast:
        received = [[h[0]] + [flipped(h[j], j) for j in range(1, PLANE)] for h in hidden]
    part = hidden_width // tiles
    if fast:
        received[0][0], received[1][0] = lax.optimization_barrier((received[0][0], received[1][0]))
        half = shape((step // 2, width), F32)
        last, pieces, order = [], [], []
        for c in range(CHUNKS):
            own, other = call(
                plane_kernel,
                (half, shape(half.shape, BF)),
                2 * PLANE * cells * step * width,
                2 * PLANE * cells * (step + width) + 2 * step * width,
                [SCALAR] + [WHOLE] * (2 * PLANE),
                scratch=[pltpu.VMEM((step, width), F32)],
                limit=12,
            )(me, *received[c], *cotangents)
            if c == 0:
                stream2, own = lax.optimization_barrier((stream2, own))
            last, more, places = reduced(own, other, c * step, last, c in DIRECT)
            pieces, order = pieces + more, order + places
        clipped = call(
            functools.partial(clip_kernel, order=order, unit=step // 2),
            shape((hidden_width, width), F32),
            4 * hidden_width * width,
            6 * hidden_width * width,
            [SCALAR] + [WHOLE] * len(pieces),
            scratch=[
                pltpu.VMEM((2 * CHUNKS * PLANE, width), F32),
                pltpu.VMEM((2 * CHUNKS * PLANE, step // 2, width), F32),
                pltpu.SemaphoreType.DMA((2 * CHUNKS * PLANE,)),
            ],
            out_spec=FAR,
            limit=24,
        )(me, *pieces)
    else:
        whole = jnp.concatenate([hidden[c][j] for j in range(PLANE) for c in range(CHUNKS)], 1)
        swapped = lax.all_to_all(
            whole.reshape(cells, tiles, part).transpose(1, 0, 2),
            "tile",
            split_axis=0,
            concat_axis=0,
            tiled=True,
        )
        gradient = call(
            gradient_kernel,
            shape((part, width), BF),
            2 * tiles * cells * part * width,
            2 * tiles * cells * (part + width),
            [WHOLE] * 2,
            limit=60,
        )(
            swapped.reshape(tiles * cells, part),
            lax.all_gather(cotangent, "tile", axis=0, tiled=True),
        )
        clipped = call(
            clip_whole_kernel,
            shape((hidden_width, width), F32),
            4 * hidden_width * width,
            6 * hidden_width * width,
            [WHOLE],
            limit=24,
        )(lax.all_gather(gradient, "tile", axis=0, tiled=True))
    latent_out = call(
        down_kernel,
        query_shape,
        2 * cells * width * hidden_width,
        2 * width * hidden_width + 2 * cells * hidden_width,
        [SCALAR] + [WHOLE] * (2 + CHUNKS * PLANE),
        limit=12,
    )(me, stream2, w_down, *[block for h in hidden for block in h])
    return (latent_out, clipped)


def solution(mesh):
    split = P(("dp", "tile"))
    rows = P(("dp", "tile"), None)
    return jax.shard_map(
        on_device,
        mesh=mesh,
        in_specs=(rows, split, rows, split, rows, P(), P(), P(), P(), P(), P(), P(), P(), rows),
        out_specs=(rows, P("dp", None)),
        check_vma=False,
    )
```

```python
import functools
import jax
import jax.numpy as jnp
from jax import lax
from jax.experimental import pallas as pl
from jax.experimental.pallas import tpu as pltpu
from jax.sharding import PartitionSpec as P

H = 8
LANES = 128
PLANE = 4
CHUNKS = 2
HOPS = ((True, True), (False, False))
BF = jnp.bfloat16
F32 = jnp.float32
MIB = 1024 * 1024
NO_KEY = -1e30


def started(sources, targets, semaphores):
    copies = [
        pltpu.make_async_copy(source, target, semaphores.at[i])
        for i, (source, target) in enumerate(zip(sources, targets, strict=True))
    ]
    for copy in copies:
        copy.start()
    return copies


def dot(a, b, dims=((1,), (0,))):
    return lax.dot_general(a, b, (dims, ((), ())), preferred_element_type=F32)


def rms_norm(values):
    return values * lax.rsqrt(jnp.mean(values * values, axis=-1, keepdims=True) + 1e-06)


def iota(shape, dim):
    return lax.broadcasted_iota(jnp.int32, shape, dim)


SCALAR = pl.BlockSpec(memory_space=pltpu.SMEM)
WHOLE = pl.BlockSpec(memory_space=pltpu.VMEM)
FAR = pl.BlockSpec(memory_space=pltpu.HBM)


def call(kernel, out_shape, flops, moved, specs, scratch=(), transcendentals=0, out_spec=None, *, limit):
    kwargs = {} if out_spec is None else {"out_specs": out_spec}
    return pl.pallas_call(
        kernel,
        out_shape=out_shape,
        **kwargs,
        in_specs=specs,
        scratch_shapes=scratch,
        compiler_params=pltpu.CompilerParams(vmem_limit_bytes=limit * MIB),
        cost_estimate=pl.CostEstimate(
            flops=flops, bytes_accessed=moved, transcendentals=transcendentals
        ),
    )


def pack_kernel(*refs, tiles, cap):
    inputs, out, local, (packed, arrivals, leaving) = refs[:5], refs[5], refs[6:11], refs[11:]
    copies = started(inputs, local, arrivals)
    route, cell, inst, table, obs = local
    rows, channels = obs.shape
    copies[0].wait()
    chosen = (iota((tiles, rows), 0) == route[...]).astype(F32)
    pieces = rows // LANES
    stacked = jnp.concatenate(
        [chosen[:, i * LANES : (i + 1) * LANES] for i in range(pieces)], axis=0
    )
    upto = (iota((LANES, LANES), 0) <= iota((LANES, LANES), 1)).astype(F32).astype(BF)
    counted = dot(stacked.astype(BF), upto)
    base = jnp.zeros((tiles, 1), F32)
    parts = []
    for i in range(pieces):
        part = counted[i * tiles : (i + 1) * tiles]
        parts.append(part + base)
        base = base + part[:, LANES - 1 :]
    place = jnp.concatenate(parts, axis=1)
    rank = (jnp.sum(chosen * place, axis=0, keepdims=True) - 1.0).astype(jnp.int32)
    slot = route[...] * cap + rank
    copies[1].wait()
    mark = chosen * (cell[...] + 1).astype(F32)
    at_rank = (iota((cap, rows), 0) == rank).astype(F32).astype(BF)
    marks = dot(mark.astype(BF), at_rank, ((1,), (1,)))
    if cap < LANES:
        marks = jnp.concatenate([marks, jnp.zeros((tiles, LANES - cap), F32)], axis=1)
    for copy in copies[2:]:
        copy.wait()
    kinds = (iota((table.shape[0], rows), 0) == inst[...]).astype(F32).astype(BF)
    embedded = (obs[...].astype(F32) + dot(kinds, table[...], ((0,), (0,)))).astype(BF)
    split = channels // LANES
    step = min(256, tiles * cap)
    sent = []
    for first in range(0, tiles * cap, step):
        pick = (iota((step, rows), 0) + first == slot).astype(F32).astype(BF)
        moved = dot(pick, embedded).astype(BF)
        here = slice(first // cap, (first + step) // cap)
        for i in range(step // cap):
            t = first // cap + i
            for c in range(split):
                packed[t, c * cap : (c + 1) * cap, :] = moved[
                    i * cap : (i + 1) * cap, c * LANES : (c + 1) * LANES
                ]
            packed[t, split * cap :, :] = jnp.broadcast_to(
                marks[t : t + 1, :], (packed.shape[1] - split * cap, LANES)
            ).astype(BF)
        sent.append(
            pltpu.make_async_copy(packed.at[here], out.at[here], leaving.at[first // step])
        )
        sent[-1].start()
    for copy in sent:
        copy.wait()


def heads_pair(query, keys, values, add, earlier=None):
    low = iota(query.shape, 1) < query.shape[1] // 2
    zero = jnp.zeros_like(query)
    lanes = query.shape[1]
    with_ones = jnp.concatenate([values, jnp.ones_like(values)], axis=1)
    results = []
    for i, q in enumerate((jnp.where(low, query, zero), jnp.where(low, zero, query))):
        scores = dot(q, keys, ((1,), (1,))) + add
        peak = jnp.max(scores, axis=1, keepdims=True)
        if earlier is not None:
            at = i * (lanes // 2)
            peak = jnp.maximum(peak, earlier[0][:, at : at + 1])
        mixed = dot(jnp.exp(scores - peak).astype(BF), with_ones)
        results.append((jnp.broadcast_to(peak, query.shape), mixed[:, :lanes], mixed[:, lanes:]))
    peak, mixed, total = (jnp.where(low, a, b) for a, b in zip(*results, strict=True))
    if earlier is not None:
        weight = jnp.exp(earlier[0] - peak)
        mixed, total = mixed + weight * earlier[1], total + weight * earlier[2]
    return peak, mixed, total


def pairs(width, body):
    for at in range(0, width, LANES):
        body(slice(at, at + LANES), slice(width + at, width + at + LANES))


def project_query(normed, weights, width):
    scaled = dot(normed, weights).astype(BF).astype(F32) * (width // H) ** -0.5
    return scaled.astype(BF)


def unpack(blocks, x, cap):
    for s, block in enumerate(blocks):
        for c in range(x.shape[1] // LANES):
            x[s * cap : (s + 1) * cap, c * LANES : (c + 1) * LANES] = block[
                c * cap : (c + 1) * cap, :
            ]


def distance(mark, cells):
    positions = iota((cells, 1), 0).astype(F32)
    return jnp.where(mark > 0.5, -4.0 * jnp.abs(positions - (mark - 1.0)) / cells, NO_KEY)


def block_marks(blocks, row):
    return jnp.concatenate([block[row : row + 1, :] for block in blocks], axis=1).astype(F32)


def query_kernel(latent, w_q, q):
    normed = rms_norm(latent[...].astype(F32)).astype(BF)
    q[...] = project_query(normed, w_q[...], q.shape[1])


def cross_kernel(*refs, cap, inputs):
    far, (stream_out, normed, top, bottom), refs = refs[:inputs], refs[inputs : inputs + 4], refs[inputs + 4 :]
    local, (x, kv, add, cross, arrivals) = refs[:inputs], refs[inputs:]
    copies = started(far, local, arrivals)
    arrived, w_kv, q, latent, w_out = local[:5]
    cells, width = latent.shape
    for i in (0, 1, *range(5, inputs)):
        copies[i].wait()
    blocks = [arrived.at[s] for s in range(arrived.shape[0])]
    unpack(blocks, x, cap)
    mark = local[5][...] if cap % LANES else block_marks(blocks, (x.shape[1] // LANES) * cap)
    kv[...] = dot(x[...], w_kv[...]).astype(BF)
    add[...] = distance(mark, cells)
    for i in (2, 3, 4):
        copies[i].wait()

    def body(at, beside):
        _, value, weight = heads_pair(q[:, at], kv[:, at], kv[:, beside], add[...])
        cross[:, at] = (value / weight).astype(BF)

    pairs(width, body)
    stream = latent[...].astype(F32) + dot(cross[...], w_out[...])
    stream_out[...] = stream
    rows = rms_norm(stream).astype(BF)
    normed[...] = rows
    top[...] = rows[: cells // 2]
    bottom[...] = rows[cells // 2 :]


def inner_kernel(w_qkv, cells_far, *refs, fetched):
    far, (q, peak, mixed, total), near = refs[:fetched], refs[fetched : fetched + 4], refs[fetched + 4 :]
    near, (kv, own, add, arrivals) = near[:fetched], near[fetched:]
    cells, width = q.shape
    reach = cells // 2
    cells_in = started((cells_far,), (own,), arrivals)
    copies = started(far, near, arrivals.at[1:]) if fetched else []
    for copy in cells_in:
        copy.wait()
    q[...] = project_query(own[...], w_qkv[:, :width], width)
    kv[...] = dot(own[...], w_qkv[:, width:]).astype(BF)
    offsets = iota(add.shape, 1) - iota(add.shape, 0)
    add[...] = jnp.where((offsets >= -reach) & (offsets <= reach), 0.0, NO_KEY)

    def body(at, beside):
        peak[:, at], mixed[:, at], total[:, at] = heads_pair(
            q[:, at], kv[:, at], kv[:, beside], add[...]
        )

    pairs(width, body)
    for copy in copies:
        copy.wait()


def outer_kernel(
    stream_in, before, after, w_qkv, w_out, q, peak, mixed, total, stream_out, normed, kv, windowed
):
    cells, width = stream_in.shape
    reach = cells // 2
    kv[:reach, :] = dot(before[...], w_qkv[:, width:]).astype(BF)
    kv[reach:, :] = dot(after[...], w_qkv[:, width:]).astype(BF)
    offsets = iota((reach, reach), 1) - iota((reach, reach), 0)
    adds = [jnp.where(seen, 0.0, NO_KEY) for seen in (offsets >= 0, offsets <= 0)]

    def body(at, beside):
        for half in range(2):
            rows = slice(half * reach, (half + 1) * reach)
            _, value, weight = heads_pair(
                q[rows, at],
                kv[rows, at],
                kv[rows, beside],
                adds[half],
                (peak[rows, at], mixed[rows, at], total[rows, at]),
            )
            windowed[rows, at] = (value / weight).astype(BF)

    pairs(width, body)
    stream = stream_in[...] + dot(windowed[...], w_out[...])
    stream_out[...] = stream
    normed[...] = rms_norm(stream).astype(BF)


def up_kernel(me, normed, w_up, *outs, chunk):
    step = outs[0].shape[1]
    for j, out in enumerate(outs):
        first = ((me[0] % PLANE) ^ j) * (CHUNKS * step) + chunk * step
        at = pl.ds(pl.multiple_of(first, step), step)
        out[...] = jax.nn.gelu(dot(normed[...], w_up[:, at])).astype(BF)


def down_kernel(me, stream, w_down, *refs):
    hidden, out = refs[:-1], refs[-1]
    step = hidden[0].shape[1]
    total = stream[...]
    for i, block in enumerate(hidden):
        chunk, j = divmod(i, PLANE)
        first = ((me[0] % PLANE) ^ j) * (CHUNKS * step) + chunk * step
        total += dot(block[...], w_down[pl.ds(pl.multiple_of(first, step), step), :])
    out[...] = total.astype(BF)


def gradient_kernel(hidden, cotangent, out):
    out[...] = dot(hidden[...], cotangent[...], ((0,), (0,))).astype(BF)


def plane_kernel(me, *refs):
    hidden, cotangent, (own, other, total) = refs[:PLANE], refs[PLANE : 2 * PLANE], refs[2 * PLANE :]
    total[...] = sum(
        dot(h[...], c[...], ((0,), (0,))) for h, c in zip(hidden, cotangent, strict=True)
    )
    rows = own.shape[0]
    for i, out in enumerate((own, other)):
        at = pl.multiple_of(((me[0] // PLANE + i) % 2) * rows, rows)
        out[...] = total[pl.ds(at, rows), :].astype(out.dtype)


def clip_kernel(me, *refs, order, unit):
    pieces, (out, sums, scaled, sent) = refs[:-4], refs[-4:]
    quarter = out.shape[0] // PLANE
    where = []
    for piece, steps in zip(pieces, order, strict=True):
        for i, (flip, base, other) in enumerate(steps):
            tile = me[0] ^ flip
            half = (tile // PLANE + other) % 2
            where.append(((tile % PLANE) * quarter + base + half * unit, piece, i))
    for at, piece, i in where:
        v = piece[i].astype(F32)
        sums[pl.ds(at // unit, 1), :] = jnp.sum(v * v, axis=0, keepdims=True)
    total = jnp.sum(jnp.sum(sums[...], axis=0, keepdims=True), axis=1, keepdims=True)
    factor = jnp.minimum(1.0, 0.5 / jnp.sqrt(total / (out.shape[0] * out.shape[1]) + 1e-06))
    copies = []
    for n, (at, piece, i) in enumerate(where):
        scaled[n] = piece[i].astype(F32) * factor
        rows = pl.ds(pl.multiple_of(at, unit), unit)
        copies.append(pltpu.make_async_copy(scaled.at[n], out.at[rows, :], sent.at[n]))
        copies[-1].start()
    for copy in copies:
        copy.wait()


def clip_whole_kernel(gradient, out):
    v = gradient[...].astype(F32)
    total = jnp.sum(jnp.sum(v * v, axis=0, keepdims=True), axis=1, keepdims=True)
    factor = jnp.minimum(1.0, 0.5 / jnp.sqrt(total / (out.shape[0] * out.shape[1]) + 1e-06))
    out[...] = v * factor


def flipped(value, k):
    return lax.ppermute(value, "tile", [(i, i ^ k) for i in range(PLANE * PLANE)])


def narrow(value):
    return value.astype(BF)


def reduced(own, other, base, hops):
    own = narrow(own + flipped(other, PLANE).astype(F32))
    own = narrow(own.astype(F32) + flipped(own, 2 * PLANE).astype(F32))
    pieces, order = [], []
    for n, (first, two) in enumerate(zip((1, 2), hops, strict=True)):
        half = flipped(own, PLANE) if n else own
        if two:
            pair = jnp.stack([half, flipped(half, first)])
            pieces += [pair, flipped(pair, 3 - first)]
            order += [[(0, base, n), (first, base, n)], [(3 - first, base, n), (3, base, n)]]
        else:
            pieces += [half[None]] + [flipped(half, j)[None] for j in range(1, PLANE)]
            order += [[(j, base, n)] for j in range(PLANE)]
    return pieces, order


def on_device(
    observations,
    instrument,
    route,
    cell_index,
    latent,
    inst_table,
    w_obs_kv,
    w_cross_q,
    w_cross_out,
    w_win_qkv,
    w_win_out,
    w_up,
    w_down,
    cotangent,
):
    tiles = lax.axis_size("tile")
    count, channels = observations.shape
    cells, width = latent.shape
    hidden_width = w_up.shape[1]
    cap = 2 * count // tiles
    split = channels // LANES
    rows = split * cap + 8
    fast = tiles == PLANE * PLANE and cap == LANES
    me = lax.axis_index("tile").reshape(1) if fast else jnp.zeros((1,), jnp.int32)
    shape = jax.ShapeDtypeStruct
    stream_shape = shape((cells, width), F32)
    half_shape = shape((cells // 2, width), BF)
    query_shape = shape((cells, width), BF)

    packed = call(
        functools.partial(pack_kernel, tiles=tiles, cap=cap),
        shape((tiles, rows, LANES), BF),
        2 * tiles * cap * count * channels,
        2 * tiles * cap * channels + 2 * count * channels,
        [FAR] * 5,
        scratch=[
            pltpu.VMEM((1, count), jnp.int32),
            pltpu.VMEM((1, count), jnp.int32),
            pltpu.VMEM((1, count), jnp.int32),
            pltpu.VMEM(inst_table.shape, BF),
            pltpu.VMEM((count, channels), BF),
            pltpu.VMEM((tiles, rows, LANES), BF),
            pltpu.SemaphoreType.DMA((5,)),
            pltpu.SemaphoreType.DMA((-(-tiles * cap // 256),)),
        ],
        out_spec=FAR,
        limit=62,
    )(
        route.reshape(1, count),
        cell_index.reshape(1, count),
        instrument.reshape(1, count),
        inst_table,
        observations,
    )

    keys = tiles * cap
    arrived = lax.all_to_all(packed, "tile", split_axis=0, concat_axis=0, tiled=True)
    if fast:
        cotangents = [flipped(cotangent, j) for j in range(1, PLANE)]
    query = call(
        query_kernel,
        query_shape,
        2 * cells * width * width,
        2 * width * width + 4 * cells * width,
        [WHOLE] * 2,
        limit=8,
    )(latent, w_cross_q)
    marks = [arrived[:, split * cap, :cap].reshape(1, keys).astype(F32)] if cap % LANES else []
    operands = (arrived, w_obs_kv, query, latent, w_cross_out, *marks)
    stream1, own, top, bottom = call(
        functools.partial(cross_kernel, cap=cap, inputs=len(operands)),
        (stream_shape, query_shape, half_shape, half_shape),
        4 * keys * channels * width + 4 * cells * keys * width,
        2 * keys * channels + 6 * width * width,
        [FAR] * len(operands),
        scratch=[pltpu.VMEM(operand.shape, operand.dtype) for operand in operands]
        + [
            pltpu.VMEM((keys, channels), BF),
            pltpu.VMEM((keys, 2 * width), BF),
            pltpu.VMEM((cells, keys), F32),
            pltpu.VMEM((cells, width), BF),
            pltpu.SemaphoreType.DMA((len(operands),)),
        ],
        transcendentals=H * cells * keys,
        limit=62,
    )(*operands)

    if not fast:
        cotangents = []
    else:
        top, bottom, *cotangents = lax.optimization_barrier((top, bottom, *cotangents))
        cotangents = [cotangent, *cotangents]
    forward = [(i, (i + 1) % tiles) for i in range(tiles)]
    backward = [(b, a) for a, b in forward]
    before = lax.ppermute(bottom, "tile", forward)
    after = lax.ppermute(top, "tile", backward)
    fetched = len(cotangents)
    partial = call(
        functools.partial(inner_kernel, fetched=fetched),
        (query_shape, stream_shape, stream_shape, stream_shape, *([query_shape] * fetched)),
        6 * cells * width * width + 4 * cells * cells * width,
        6 * width * width + 16 * cells * width,
        [WHOLE] + [FAR] * (1 + fetched),
        scratch=[
            pltpu.VMEM((cells, 2 * width), BF),
            pltpu.VMEM((cells, width), BF),
            pltpu.VMEM((cells, cells), F32),
            pltpu.SemaphoreType.DMA((1 + fetched,)),
        ],
        transcendentals=H * cells * cells,
        limit=20,
    )(w_win_qkv, own, *cotangents)
    partial, cotangents = partial[:4], partial[4:]
    stream2, normed = call(
        outer_kernel,
        (stream_shape, query_shape),
        6 * cells * width * width + 2 * cells * cells * width,
        8 * width * width + 24 * cells * width,
        [WHOLE] * 9,
        scratch=[pltpu.VMEM((cells, 2 * width), BF), pltpu.VMEM((cells, width), BF)],
        transcendentals=H * cells * cells // 2,
        limit=20,
    )(stream1, before, after, w_win_qkv, w_win_out, *partial)

    step = hidden_width // (CHUNKS * PLANE)
    hidden = [
        call(
            functools.partial(up_kernel, chunk=c),
            [shape((cells, step), BF)] * PLANE,
            2 * cells * width * hidden_width // CHUNKS,
            2 * width * hidden_width // CHUNKS + 2 * cells * hidden_width // CHUNKS,
            [SCALAR, WHOLE, WHOLE],
            transcendentals=cells * hidden_width // CHUNKS,
            limit=12,
        )(me, normed, w_up)
        for c in range(CHUNKS)
    ]
    if fast:
        received = [[h[0]] + [flipped(h[j], j) for j in range(1, PLANE)] for h in hidden]
    part = hidden_width // tiles
    if fast:
        received[0][0], received[1][0] = lax.optimization_barrier((received[0][0], received[1][0]))
        half = shape((step // 2, width), F32)
        pieces, order = [], []
        for c in range(CHUNKS):
            own, other = call(
                plane_kernel,
                (half, shape(half.shape, BF)),
                2 * PLANE * cells * step * width,
                2 * PLANE * cells * (step + width) + 2 * step * width,
                [SCALAR] + [WHOLE] * (2 * PLANE),
                scratch=[pltpu.VMEM((step, width), F32)],
                limit=12,
            )(me, *received[c], *cotangents)
            if c == 0:
                stream2, own = lax.optimization_barrier((stream2, own))
            more, places = reduced(own, other, c * step, HOPS[c])
            pieces, order = pieces + more, order + places
        clipped = call(
            functools.partial(clip_kernel, order=order, unit=step // 2),
            shape((hidden_width, width), F32),
            4 * hidden_width * width,
            6 * hidden_width * width,
            [SCALAR] + [WHOLE] * len(pieces),
            scratch=[
                pltpu.VMEM((2 * CHUNKS * PLANE, width), F32),
                pltpu.VMEM((2 * CHUNKS * PLANE, step // 2, width), F32),
                pltpu.SemaphoreType.DMA((2 * CHUNKS * PLANE,)),
            ],
            out_spec=FAR,
            limit=24,
        )(me, *pieces)
    else:
        whole = jnp.concatenate([hidden[c][j] for j in range(PLANE) for c in range(CHUNKS)], 1)
        swapped = lax.all_to_all(
            whole.reshape(cells, tiles, part).transpose(1, 0, 2),
            "tile",
            split_axis=0,
            concat_axis=0,
            tiled=True,
        )
        gradient = call(
            gradient_kernel,
            shape((part, width), BF),
            2 * tiles * cells * part * width,
            2 * tiles * cells * (part + width),
            [WHOLE] * 2,
            limit=60,
        )(
            swapped.reshape(tiles * cells, part),
            lax.all_gather(cotangent, "tile", axis=0, tiled=True),
        )
        clipped = call(
            clip_whole_kernel,
            shape((hidden_width, width), F32),
            4 * hidden_width * width,
            6 * hidden_width * width,
            [WHOLE],
            limit=24,
        )(lax.all_gather(gradient, "tile", axis=0, tiled=True))
    latent_out = call(
        down_kernel,
        query_shape,
        2 * cells * width * hidden_width,
        2 * width * hidden_width + 2 * cells * hidden_width,
        [SCALAR] + [WHOLE] * (2 + CHUNKS * PLANE),
        limit=12,
    )(me, stream2, w_down, *[block for h in hidden for block in h])
    return (latent_out, clipped)


def solution(mesh):
    split = P(("dp", "tile"))
    rows = P(("dp", "tile"), None)
    return jax.shard_map(
        on_device,
        mesh=mesh,
        in_specs=(rows, split, rows, split, rows, P(), P(), P(), P(), P(), P(), P(), P(), rows),
        out_specs=(rows, P("dp", None)),
        check_vma=False,
    )
```

```python
import functools
import jax
import jax.numpy as jnp
from jax import lax
from jax.experimental import pallas as pl
from jax.experimental.pallas import tpu as pltpu
from jax.sharding import PartitionSpec as P

H = 8
LANES = 128
PLANE = 4
CHUNKS = 2
HOPS = ((True, True), (False, False))
BF = jnp.bfloat16
F32 = jnp.float32
MIB = 1024 * 1024
NO_KEY = -1e30


def started(sources, targets, semaphores):
    copies = [
        pltpu.make_async_copy(source, target, semaphores.at[i])
        for i, (source, target) in enumerate(zip(sources, targets, strict=True))
    ]
    for copy in copies:
        copy.start()
    return copies


def dot(a, b, dims=((1,), (0,))):
    return lax.dot_general(a, b, (dims, ((), ())), preferred_element_type=F32)


def rms_norm(values):
    return values * lax.rsqrt(jnp.mean(values * values, axis=-1, keepdims=True) + 1e-06)


def iota(shape, dim):
    return lax.broadcasted_iota(jnp.int32, shape, dim)


SCALAR = pl.BlockSpec(memory_space=pltpu.SMEM)
WHOLE = pl.BlockSpec(memory_space=pltpu.VMEM)
FAR = pl.BlockSpec(memory_space=pltpu.HBM)


def call(kernel, out_shape, flops, moved, specs, scratch=(), transcendentals=0, out_spec=None, *, limit):
    kwargs = {} if out_spec is None else {"out_specs": out_spec}
    return pl.pallas_call(
        kernel,
        out_shape=out_shape,
        **kwargs,
        in_specs=specs,
        scratch_shapes=scratch,
        compiler_params=pltpu.CompilerParams(vmem_limit_bytes=limit * MIB),
        cost_estimate=pl.CostEstimate(
            flops=flops, bytes_accessed=moved, transcendentals=transcendentals
        ),
    )


def pack_kernel(*refs, tiles, cap):
    inputs, out, local, (packed, arrivals, leaving) = refs[:5], refs[5], refs[6:11], refs[11:]
    copies = started(inputs, local, arrivals)
    route, cell, inst, table, obs = local
    rows, channels = obs.shape
    copies[0].wait()
    chosen = (iota((tiles, rows), 0) == route[...]).astype(F32)
    pieces = rows // LANES
    stacked = jnp.concatenate(
        [chosen[:, i * LANES : (i + 1) * LANES] for i in range(pieces)], axis=0
    )
    upto = (iota((LANES, LANES), 0) <= iota((LANES, LANES), 1)).astype(F32).astype(BF)
    counted = dot(stacked.astype(BF), upto)
    base = jnp.zeros((tiles, 1), F32)
    parts = []
    for i in range(pieces):
        part = counted[i * tiles : (i + 1) * tiles]
        parts.append(part + base)
        base = base + part[:, LANES - 1 :]
    place = jnp.concatenate(parts, axis=1)
    rank = (jnp.sum(chosen * place, axis=0, keepdims=True) - 1.0).astype(jnp.int32)
    slot = route[...] * cap + rank
    copies[1].wait()
    mark = chosen * (cell[...] + 1).astype(F32)
    at_rank = (iota((cap, rows), 0) == rank).astype(F32).astype(BF)
    marks = dot(mark.astype(BF), at_rank, ((1,), (1,)))
    if cap < LANES:
        marks = jnp.concatenate([marks, jnp.zeros((tiles, LANES - cap), F32)], axis=1)
    for copy in copies[2:]:
        copy.wait()
    kinds = (iota((table.shape[0], rows), 0) == inst[...]).astype(F32).astype(BF)
    embedded = (obs[...].astype(F32) + dot(kinds, table[...], ((0,), (0,)))).astype(BF)
    split = channels // LANES
    step = min(256, tiles * cap)
    sent = []
    for first in range(0, tiles * cap, step):
        pick = (iota((step, rows), 0) + first == slot).astype(F32).astype(BF)
        moved = dot(pick, embedded).astype(BF)
        here = slice(first // cap, (first + step) // cap)
        for i in range(step // cap):
            t = first // cap + i
            for c in range(split):
                packed[t, c * cap : (c + 1) * cap, :] = moved[
                    i * cap : (i + 1) * cap, c * LANES : (c + 1) * LANES
                ]
            packed[t, split * cap :, :] = jnp.broadcast_to(
                marks[t : t + 1, :], (packed.shape[1] - split * cap, LANES)
            ).astype(BF)
        sent.append(
            pltpu.make_async_copy(packed.at[here], out.at[here], leaving.at[first // step])
        )
        sent[-1].start()
    for copy in sent:
        copy.wait()


def heads_pair(query, keys, values, add, earlier=None):
    low = iota(query.shape, 1) < query.shape[1] // 2
    zero = jnp.zeros_like(query)
    lanes = query.shape[1]
    with_ones = jnp.concatenate([values, jnp.ones_like(values)], axis=1)
    results = []
    for i, q in enumerate((jnp.where(low, query, zero), jnp.where(low, zero, query))):
        scores = dot(q, keys, ((1,), (1,))) + add
        peak = jnp.max(scores, axis=1, keepdims=True)
        if earlier is not None:
            at = i * (lanes // 2)
            peak = jnp.maximum(peak, earlier[0][:, at : at + 1])
        mixed = dot(jnp.exp(scores - peak).astype(BF), with_ones)
        results.append((jnp.broadcast_to(peak, query.shape), mixed[:, :lanes], mixed[:, lanes:]))
    peak, mixed, total = (jnp.where(low, a, b) for a, b in zip(*results, strict=True))
    if earlier is not None:
        weight = jnp.exp(earlier[0] - peak)
        mixed, total = mixed + weight * earlier[1], total + weight * earlier[2]
    return peak, mixed, total


def pairs(width, body):
    for at in range(0, width, LANES):
        body(slice(at, at + LANES), slice(width + at, width + at + LANES))


def project_query(normed, weights, width):
    scaled = dot(normed, weights).astype(BF).astype(F32) * (width // H) ** -0.5
    return scaled.astype(BF)


def unpack(blocks, x, cap):
    for s, block in enumerate(blocks):
        for c in range(x.shape[1] // LANES):
            x[s * cap : (s + 1) * cap, c * LANES : (c + 1) * LANES] = block[
                c * cap : (c + 1) * cap, :
            ]


def distance(mark, cells):
    positions = iota((cells, 1), 0).astype(F32)
    return jnp.where(mark > 0.5, -4.0 * jnp.abs(positions - (mark - 1.0)) / cells, NO_KEY)


def block_marks(blocks, row):
    return jnp.concatenate([block[row : row + 1, :] for block in blocks], axis=1).astype(F32)


def query_kernel(latent, w_q, q):
    normed = rms_norm(latent[...].astype(F32)).astype(BF)
    q[...] = project_query(normed, w_q[...], q.shape[1])


def cross_kernel(*refs, cap, inputs):
    far, (stream_out, normed, top, bottom), refs = refs[:inputs], refs[inputs : inputs + 4], refs[inputs + 4 :]
    local, (x, kv, add, cross, arrivals) = refs[:inputs], refs[inputs:]
    copies = started(far, local, arrivals)
    arrived, w_kv, q, latent, w_out = local[:5]
    cells, width = latent.shape
    for i in (0, 1, *range(5, inputs)):
        copies[i].wait()
    blocks = [arrived.at[s] for s in range(arrived.shape[0])]
    unpack(blocks, x, cap)
    mark = local[5][...] if cap % LANES else block_marks(blocks, (x.shape[1] // LANES) * cap)
    kv[...] = dot(x[...], w_kv[...]).astype(BF)
    add[...] = distance(mark, cells)
    for i in (2, 3, 4):
        copies[i].wait()

    def body(at, beside):
        _, value, weight = heads_pair(q[:, at], kv[:, at], kv[:, beside], add[...])
        cross[:, at] = (value / weight).astype(BF)

    pairs(width, body)
    stream = latent[...].astype(F32) + dot(cross[...], w_out[...])
    stream_out[...] = stream
    rows = rms_norm(stream).astype(BF)
    normed[...] = rows
    top[...] = rows[: cells // 2]
    bottom[...] = rows[cells // 2 :]


def inner_kernel(w_qkv, cells_far, *refs, fetched):
    far, (q, peak, mixed, total), near = refs[:fetched], refs[fetched : fetched + 4], refs[fetched + 4 :]
    near, (kv, own, add, arrivals) = near[:fetched], near[fetched:]
    cells, width = q.shape
    reach = cells // 2
    cells_in = started((cells_far,), (own,), arrivals)
    copies = started(far, near, arrivals.at[1:]) if fetched else []
    for copy in cells_in:
        copy.wait()
    q[...] = project_query(own[...], w_qkv[:, :width], width)
    kv[...] = dot(own[...], w_qkv[:, width:]).astype(BF)
    offsets = iota(add.shape, 1) - iota(add.shape, 0)
    add[...] = jnp.where((offsets >= -reach) & (offsets <= reach), 0.0, NO_KEY)

    def body(at, beside):
        peak[:, at], mixed[:, at], total[:, at] = heads_pair(
            q[:, at], kv[:, at], kv[:, beside], add[...]
        )

    pairs(width, body)
    for copy in copies:
        copy.wait()


def outer_kernel(
    stream_in, before, after, w_qkv, w_out, q, peak, mixed, total, stream_out, normed, kv, windowed
):
    cells, width = stream_in.shape
    reach = cells // 2
    kv[:reach, :] = dot(before[...], w_qkv[:, width:]).astype(BF)
    kv[reach:, :] = dot(after[...], w_qkv[:, width:]).astype(BF)
    offsets = iota((reach, reach), 1) - iota((reach, reach), 0)
    adds = [jnp.where(seen, 0.0, NO_KEY) for seen in (offsets >= 0, offsets <= 0)]

    def body(at, beside):
        for half in range(2):
            rows = slice(half * reach, (half + 1) * reach)
            _, value, weight = heads_pair(
                q[rows, at],
                kv[rows, at],
                kv[rows, beside],
                adds[half],
                (peak[rows, at], mixed[rows, at], total[rows, at]),
            )
            windowed[rows, at] = (value / weight).astype(BF)

    pairs(width, body)
    stream = stream_in[...] + dot(windowed[...], w_out[...])
    stream_out[...] = stream
    normed[...] = rms_norm(stream).astype(BF)


def up_kernel(me, normed, w_up, *outs, chunk):
    step = outs[0].shape[1]
    for j, out in enumerate(outs):
        first = ((me[0] % PLANE) ^ j) * (CHUNKS * step) + chunk * step
        at = pl.ds(pl.multiple_of(first, step), step)
        out[...] = jax.nn.gelu(dot(normed[...], w_up[:, at])).astype(BF)


def down_kernel(me, stream, w_down, *refs):
    hidden, out = refs[:-1], refs[-1]
    step = hidden[0].shape[1]
    total = stream[...]
    for i, block in enumerate(hidden):
        chunk, j = divmod(i, PLANE)
        first = ((me[0] % PLANE) ^ j) * (CHUNKS * step) + chunk * step
        total += dot(block[...], w_down[pl.ds(pl.multiple_of(first, step), step), :])
    out[...] = total.astype(BF)


def gradient_kernel(hidden, cotangent, out):
    out[...] = dot(hidden[...], cotangent[...], ((0,), (0,))).astype(BF)


def plane_kernel(me, *refs):
    hidden, cotangent, (own, other, total) = refs[:PLANE], refs[PLANE : 2 * PLANE], refs[2 * PLANE :]
    total[...] = sum(
        dot(h[...], c[...], ((0,), (0,))) for h, c in zip(hidden, cotangent, strict=True)
    )
    rows = own.shape[0]
    for i, out in enumerate((own, other)):
        at = pl.multiple_of(((me[0] // PLANE + i) % 2) * rows, rows)
        out[...] = total[pl.ds(at, rows), :].astype(out.dtype)


def clip_kernel(me, *refs, order, unit):
    pieces, (out, sums, scaled, sent) = refs[:-4], refs[-4:]
    quarter = out.shape[0] // PLANE
    where = []
    for piece, steps in zip(pieces, order, strict=True):
        for i, (flip, base, other) in enumerate(steps):
            tile = me[0] ^ flip
            half = (tile // PLANE + other) % 2
            where.append(((tile % PLANE) * quarter + base + half * unit, piece, i))
    for at, piece, i in where:
        v = piece[i].astype(F32)
        sums[pl.ds(at // unit, 1), :] = jnp.sum(v * v, axis=0, keepdims=True)
    total = jnp.sum(jnp.sum(sums[...], axis=0, keepdims=True), axis=1, keepdims=True)
    factor = jnp.minimum(1.0, 0.5 / jnp.sqrt(total / (out.shape[0] * out.shape[1]) + 1e-06))
    copies = []
    for n, (at, piece, i) in enumerate(where):
        scaled[n] = piece[i].astype(F32) * factor
        rows = pl.ds(pl.multiple_of(at, unit), unit)
        copies.append(pltpu.make_async_copy(scaled.at[n], out.at[rows, :], sent.at[n]))
        copies[-1].start()
    for copy in copies:
        copy.wait()


def clip_whole_kernel(gradient, out):
    v = gradient[...].astype(F32)
    total = jnp.sum(jnp.sum(v * v, axis=0, keepdims=True), axis=1, keepdims=True)
    factor = jnp.minimum(1.0, 0.5 / jnp.sqrt(total / (out.shape[0] * out.shape[1]) + 1e-06))
    out[...] = v * factor


def flipped(value, k):
    return lax.ppermute(value, "tile", [(i, i ^ k) for i in range(PLANE * PLANE)])


def narrow(value):
    return value.astype(BF)


def reduced(own, other, base, hops):
    own = narrow(own + flipped(other, PLANE).astype(F32))
    own = narrow(own.astype(F32) + flipped(own, 2 * PLANE).astype(F32))
    pieces, order = [], []
    for n, (first, two) in enumerate(zip((1, 2), hops, strict=True)):
        half = flipped(own, PLANE) if n else own
        if two:
            pair = jnp.stack([half, flipped(half, first)])
            pieces += [pair, flipped(pair, 3 - first)]
            order += [[(0, base, n), (first, base, n)], [(3 - first, base, n), (3, base, n)]]
        else:
            pieces += [half[None]] + [flipped(half, j)[None] for j in range(1, PLANE)]
            order += [[(j, base, n)] for j in range(PLANE)]
    return pieces, order


def on_device(
    observations,
    instrument,
    route,
    cell_index,
    latent,
    inst_table,
    w_obs_kv,
    w_cross_q,
    w_cross_out,
    w_win_qkv,
    w_win_out,
    w_up,
    w_down,
    cotangent,
):
    tiles = lax.axis_size("tile")
    count, channels = observations.shape
    cells, width = latent.shape
    hidden_width = w_up.shape[1]
    cap = 2 * count // tiles
    split = channels // LANES
    rows = split * cap + 8
    fast = tiles == PLANE * PLANE and cap == LANES
    me = lax.axis_index("tile").reshape(1) if fast else jnp.zeros((1,), jnp.int32)
    shape = jax.ShapeDtypeStruct
    stream_shape = shape((cells, width), F32)
    half_shape = shape((cells // 2, width), BF)
    query_shape = shape((cells, width), BF)

    packed = call(
        functools.partial(pack_kernel, tiles=tiles, cap=cap),
        shape((tiles, rows, LANES), BF),
        2 * tiles * cap * count * channels,
        2 * tiles * cap * channels + 2 * count * channels,
        [FAR] * 5,
        scratch=[
            pltpu.VMEM((1, count), jnp.int32),
            pltpu.VMEM((1, count), jnp.int32),
            pltpu.VMEM((1, count), jnp.int32),
            pltpu.VMEM(inst_table.shape, BF),
            pltpu.VMEM((count, channels), BF),
            pltpu.VMEM((tiles, rows, LANES), BF),
            pltpu.SemaphoreType.DMA((5,)),
            pltpu.SemaphoreType.DMA((-(-tiles * cap // 256),)),
        ],
        out_spec=FAR,
        limit=62,
    )(
        route.reshape(1, count),
        cell_index.reshape(1, count),
        instrument.reshape(1, count),
        inst_table,
        observations,
    )

    keys = tiles * cap
    arrived = lax.all_to_all(packed, "tile", split_axis=0, concat_axis=0, tiled=True)
    if fast:
        cotangents = [flipped(cotangent, j) for j in range(1, PLANE)]
    query = call(
        query_kernel,
        query_shape,
        2 * cells * width * width,
        2 * width * width + 4 * cells * width,
        [WHOLE] * 2,
        limit=8,
    )(latent, w_cross_q)
    marks = [arrived[:, split * cap, :cap].reshape(1, keys).astype(F32)] if cap % LANES else []
    operands = (arrived, w_obs_kv, query, latent, w_cross_out, *marks)
    stream1, own, top, bottom = call(
        functools.partial(cross_kernel, cap=cap, inputs=len(operands)),
        (stream_shape, query_shape, half_shape, half_shape),
        4 * keys * channels * width + 4 * cells * keys * width,
        2 * keys * channels + 6 * width * width,
        [FAR] * len(operands),
        scratch=[pltpu.VMEM(operand.shape, operand.dtype) for operand in operands]
        + [
            pltpu.VMEM((keys, channels), BF),
            pltpu.VMEM((keys, 2 * width), BF),
            pltpu.VMEM((cells, keys), F32),
            pltpu.VMEM((cells, width), BF),
            pltpu.SemaphoreType.DMA((len(operands),)),
        ],
        transcendentals=H * cells * keys,
        limit=62,
    )(*operands)

    if not fast:
        cotangents = []
    else:
        top, bottom, *cotangents = lax.optimization_barrier((top, bottom, *cotangents))
        cotangents = [cotangent, *cotangents]
    forward = [(i, (i + 1) % tiles) for i in range(tiles)]
    backward = [(b, a) for a, b in forward]
    before = lax.ppermute(bottom, "tile", forward)
    after = lax.ppermute(top, "tile", backward)
    fetched = len(cotangents)
    partial = call(
        functools.partial(inner_kernel, fetched=fetched),
        (query_shape, stream_shape, stream_shape, stream_shape, *([query_shape] * fetched)),
        6 * cells * width * width + 4 * cells * cells * width,
        6 * width * width + 16 * cells * width,
        [WHOLE] + [FAR] * (1 + fetched),
        scratch=[
            pltpu.VMEM((cells, 2 * width), BF),
            pltpu.VMEM((cells, width), BF),
            pltpu.VMEM((cells, cells), F32),
            pltpu.SemaphoreType.DMA((1 + fetched,)),
        ],
        transcendentals=H * cells * cells,
        limit=20,
    )(w_win_qkv, own, *cotangents)
    partial, cotangents = partial[:4], partial[4:]
    stream2, normed = call(
        outer_kernel,
        (stream_shape, query_shape),
        6 * cells * width * width + 2 * cells * cells * width,
        8 * width * width + 24 * cells * width,
        [WHOLE] * 9,
        scratch=[pltpu.VMEM((cells, 2 * width), BF), pltpu.VMEM((cells, width), BF)],
        transcendentals=H * cells * cells // 2,
        limit=20,
    )(stream1, before, after, w_win_qkv, w_win_out, *partial)

    step = hidden_width // (CHUNKS * PLANE)
    hidden = [
        call(
            functools.partial(up_kernel, chunk=c),
            [shape((cells, step), BF)] * PLANE,
            2 * cells * width * hidden_width // CHUNKS,
            2 * width * hidden_width // CHUNKS + 2 * cells * hidden_width // CHUNKS,
            [SCALAR, WHOLE, WHOLE],
            transcendentals=cells * hidden_width // CHUNKS,
            limit=12,
        )(me, normed, w_up)
        for c in range(CHUNKS)
    ]
    if fast:
        received = [[h[0]] + [flipped(h[j], j) for j in range(1, PLANE)] for h in hidden]
    part = hidden_width // tiles
    if fast:
        half = shape((step // 2, width), F32)
        pieces, order = [], []
        for c in range(CHUNKS):
            own, other = call(
                plane_kernel,
                (half, shape(half.shape, BF)),
                2 * PLANE * cells * step * width,
                2 * PLANE * cells * (step + width) + 2 * step * width,
                [SCALAR] + [WHOLE] * (2 * PLANE),
                scratch=[pltpu.VMEM((step, width), F32)],
                limit=12,
            )(me, *received[c], *cotangents)
            if c == 0:
                stream2, own = lax.optimization_barrier((stream2, own))
            more, places = reduced(own, other, c * step, HOPS[c])
            pieces, order = pieces + more, order + places
        clipped = call(
            functools.partial(clip_kernel, order=order, unit=step // 2),
            shape((hidden_width, width), F32),
            4 * hidden_width * width,
            6 * hidden_width * width,
            [SCALAR] + [WHOLE] * len(pieces),
            scratch=[
                pltpu.VMEM((2 * CHUNKS * PLANE, width), F32),
                pltpu.VMEM((2 * CHUNKS * PLANE, step // 2, width), F32),
                pltpu.SemaphoreType.DMA((2 * CHUNKS * PLANE,)),
            ],
            out_spec=FAR,
            limit=24,
        )(me, *pieces)
    else:
        whole = jnp.concatenate([hidden[c][j] for j in range(PLANE) for c in range(CHUNKS)], 1)
        swapped = lax.all_to_all(
            whole.reshape(cells, tiles, part).transpose(1, 0, 2),
            "tile",
            split_axis=0,
            concat_axis=0,
            tiled=True,
        )
        gradient = call(
            gradient_kernel,
            shape((part, width), BF),
            2 * tiles * cells * part * width,
            2 * tiles * cells * (part + width),
            [WHOLE] * 2,
            limit=60,
        )(
            swapped.reshape(tiles * cells, part),
            lax.all_gather(cotangent, "tile", axis=0, tiled=True),
        )
        clipped = call(
            clip_whole_kernel,
            shape((hidden_width, width), F32),
            4 * hidden_width * width,
            6 * hidden_width * width,
            [WHOLE],
            limit=24,
        )(lax.all_gather(gradient, "tile", axis=0, tiled=True))
    latent_out = call(
        down_kernel,
        query_shape,
        2 * cells * width * hidden_width,
        2 * width * hidden_width + 2 * cells * hidden_width,
        [SCALAR] + [WHOLE] * (2 + CHUNKS * PLANE),
        limit=12,
    )(me, stream2, w_down, *[block for h in hidden for block in h])
    return (latent_out, clipped)


def solution(mesh):
    split = P(("dp", "tile"))
    rows = P(("dp", "tile"), None)
    return jax.shard_map(
        on_device,
        mesh=mesh,
        in_specs=(rows, split, rows, split, rows, P(), P(), P(), P(), P(), P(), P(), P(), rows),
        out_specs=(rows, P("dp", None)),
        check_vma=False,
    )
```

```python
import functools
import jax
import jax.numpy as jnp
from jax import lax
from jax.experimental import pallas as pl
from jax.experimental.pallas import tpu as pltpu
from jax.sharding import PartitionSpec as P

H = 8
LANES = 128
PLANE = 4
CHUNKS = 2
HOPS = ((True, True), (False, False))
BF = jnp.bfloat16
F32 = jnp.float32
MIB = 1024 * 1024
NO_KEY = -1e30


def started(sources, targets, semaphores):
    copies = [
        pltpu.make_async_copy(source, target, semaphores.at[i])
        for i, (source, target) in enumerate(zip(sources, targets, strict=True))
    ]
    for copy in copies:
        copy.start()
    return copies


def dot(a, b, dims=((1,), (0,))):
    return lax.dot_general(a, b, (dims, ((), ())), preferred_element_type=F32)


def rms_norm(values):
    return values * lax.rsqrt(jnp.mean(values * values, axis=-1, keepdims=True) + 1e-06)


def iota(shape, dim):
    return lax.broadcasted_iota(jnp.int32, shape, dim)


SCALAR = pl.BlockSpec(memory_space=pltpu.SMEM)
WHOLE = pl.BlockSpec(memory_space=pltpu.VMEM)
FAR = pl.BlockSpec(memory_space=pltpu.HBM)


def call(kernel, out_shape, flops, moved, specs, scratch=(), transcendentals=0, out_spec=None, *, limit):
    kwargs = {} if out_spec is None else {"out_specs": out_spec}
    return pl.pallas_call(
        kernel,
        out_shape=out_shape,
        **kwargs,
        in_specs=specs,
        scratch_shapes=scratch,
        compiler_params=pltpu.CompilerParams(vmem_limit_bytes=limit * MIB),
        cost_estimate=pl.CostEstimate(
            flops=flops, bytes_accessed=moved, transcendentals=transcendentals
        ),
    )


def pack_kernel(*refs, tiles, cap):
    inputs, out, local, (packed, arrivals, leaving) = refs[:5], refs[5], refs[6:11], refs[11:]
    copies = started(inputs, local, arrivals)
    route, cell, inst, table, obs = local
    rows, channels = obs.shape
    copies[0].wait()
    chosen = (iota((tiles, rows), 0) == route[...]).astype(F32)
    pieces = rows // LANES
    stacked = jnp.concatenate(
        [chosen[:, i * LANES : (i + 1) * LANES] for i in range(pieces)], axis=0
    )
    upto = (iota((LANES, LANES), 0) <= iota((LANES, LANES), 1)).astype(F32).astype(BF)
    counted = dot(stacked.astype(BF), upto)
    base = jnp.zeros((tiles, 1), F32)
    parts = []
    for i in range(pieces):
        part = counted[i * tiles : (i + 1) * tiles]
        parts.append(part + base)
        base = base + part[:, LANES - 1 :]
    place = jnp.concatenate(parts, axis=1)
    rank = (jnp.sum(chosen * place, axis=0, keepdims=True) - 1.0).astype(jnp.int32)
    slot = route[...] * cap + rank
    copies[1].wait()
    mark = chosen * (cell[...] + 1).astype(F32)
    at_rank = (iota((cap, rows), 0) == rank).astype(F32).astype(BF)
    marks = dot(mark.astype(BF), at_rank, ((1,), (1,)))
    if cap < LANES:
        marks = jnp.concatenate([marks, jnp.zeros((tiles, LANES - cap), F32)], axis=1)
    for copy in copies[2:]:
        copy.wait()
    kinds = (iota((table.shape[0], rows), 0) == inst[...]).astype(F32).astype(BF)
    embedded = (obs[...].astype(F32) + dot(kinds, table[...], ((0,), (0,)))).astype(BF)
    split = channels // LANES
    step = min(256, tiles * cap)
    sent = []
    for first in range(0, tiles * cap, step):
        pick = (iota((step, rows), 0) + first == slot).astype(F32).astype(BF)
        moved = dot(pick, embedded).astype(BF)
        here = slice(first // cap, (first + step) // cap)
        for i in range(step // cap):
            t = first // cap + i
            for c in range(split):
                packed[t, c * cap : (c + 1) * cap, :] = moved[
                    i * cap : (i + 1) * cap, c * LANES : (c + 1) * LANES
                ]
            packed[t, split * cap :, :] = jnp.broadcast_to(
                marks[t : t + 1, :], (packed.shape[1] - split * cap, LANES)
            ).astype(BF)
        sent.append(
            pltpu.make_async_copy(packed.at[here], out.at[here], leaving.at[first // step])
        )
        sent[-1].start()
    for copy in sent:
        copy.wait()


def heads_pair(query, keys, values, add, earlier=None):
    low = iota(query.shape, 1) < query.shape[1] // 2
    zero = jnp.zeros_like(query)
    lanes = query.shape[1]
    with_ones = jnp.concatenate([values, jnp.ones_like(values)], axis=1)
    results = []
    for i, q in enumerate((jnp.where(low, query, zero), jnp.where(low, zero, query))):
        scores = dot(q, keys, ((1,), (1,))) + add
        peak = jnp.max(scores, axis=1, keepdims=True)
        if earlier is not None:
            at = i * (lanes // 2)
            peak = jnp.maximum(peak, earlier[0][:, at : at + 1])
        mixed = dot(jnp.exp(scores - peak).astype(BF), with_ones)
        results.append((jnp.broadcast_to(peak, query.shape), mixed[:, :lanes], mixed[:, lanes:]))
    peak, mixed, total = (jnp.where(low, a, b) for a, b in zip(*results, strict=True))
    if earlier is not None:
        weight = jnp.exp(earlier[0] - peak)
        mixed, total = mixed + weight * earlier[1], total + weight * earlier[2]
    return peak, mixed, total


def pairs(width, body):
    for at in range(0, width, LANES):
        body(slice(at, at + LANES), slice(width + at, width + at + LANES))


def project_query(normed, weights, width):
    scaled = dot(normed, weights).astype(BF).astype(F32) * (width // H) ** -0.5
    return scaled.astype(BF)


def unpack(blocks, x, cap):
    for s, block in enumerate(blocks):
        for c in range(x.shape[1] // LANES):
            x[s * cap : (s + 1) * cap, c * LANES : (c + 1) * LANES] = block[
                c * cap : (c + 1) * cap, :
            ]


def distance(mark, cells):
    positions = iota((cells, 1), 0).astype(F32)
    return jnp.where(mark > 0.5, -4.0 * jnp.abs(positions - (mark - 1.0)) / cells, NO_KEY)


def block_marks(blocks, row):
    return jnp.concatenate([block[row : row + 1, :] for block in blocks], axis=1).astype(F32)


def query_kernel(latent, w_q, q):
    normed = rms_norm(latent[...].astype(F32)).astype(BF)
    q[...] = project_query(normed, w_q[...], q.shape[1])


def cross_kernel(*refs, cap, inputs):
    far, (stream_out, normed, top, bottom), refs = refs[:inputs], refs[inputs : inputs + 4], refs[inputs + 4 :]
    local, (x, kv, add, cross, arrivals) = refs[:inputs], refs[inputs:]
    copies = started(far, local, arrivals)
    arrived, w_kv, q, latent, w_out = local[:5]
    cells, width = latent.shape
    for i in (0, 1, *range(5, inputs)):
        copies[i].wait()
    blocks = [arrived.at[s] for s in range(arrived.shape[0])]
    unpack(blocks, x, cap)
    mark = local[5][...] if cap % LANES else block_marks(blocks, (x.shape[1] // LANES) * cap)
    kv[...] = dot(x[...], w_kv[...]).astype(BF)
    add[...] = distance(mark, cells)
    for i in (2, 3, 4):
        copies[i].wait()

    def body(at, beside):
        _, value, weight = heads_pair(q[:, at], kv[:, at], kv[:, beside], add[...])
        cross[:, at] = (value / weight).astype(BF)

    pairs(width, body)
    stream = latent[...].astype(F32) + dot(cross[...], w_out[...])
    stream_out[...] = stream
    rows = rms_norm(stream).astype(BF)
    normed[...] = rows
    top[...] = rows[: cells // 2]
    bottom[...] = rows[cells // 2 :]


def inner_kernel(w_qkv, cells_far, *refs, fetched):
    far, (q, peak, mixed, total), near = refs[:fetched], refs[fetched : fetched + 4], refs[fetched + 4 :]
    near, (kv, own, add, arrivals) = near[:fetched], near[fetched:]
    cells, width = q.shape
    reach = cells // 2
    cells_in = started((cells_far,), (own,), arrivals)
    copies = started(far, near, arrivals.at[1:]) if fetched else []
    for copy in cells_in:
        copy.wait()
    q[...] = project_query(own[...], w_qkv[:, :width], width)
    kv[...] = dot(own[...], w_qkv[:, width:]).astype(BF)
    offsets = iota(add.shape, 1) - iota(add.shape, 0)
    add[...] = jnp.where((offsets >= -reach) & (offsets <= reach), 0.0, NO_KEY)

    def body(at, beside):
        peak[:, at], mixed[:, at], total[:, at] = heads_pair(
            q[:, at], kv[:, at], kv[:, beside], add[...]
        )

    pairs(width, body)
    for copy in copies:
        copy.wait()


def outer_kernel(
    stream_in, before, after, w_qkv, w_out, q, peak, mixed, total, stream_out, normed, kv, windowed
):
    cells, width = stream_in.shape
    reach = cells // 2
    kv[:reach, :] = dot(before[...], w_qkv[:, width:]).astype(BF)
    kv[reach:, :] = dot(after[...], w_qkv[:, width:]).astype(BF)
    offsets = iota((reach, reach), 1) - iota((reach, reach), 0)
    adds = [jnp.where(seen, 0.0, NO_KEY) for seen in (offsets >= 0, offsets <= 0)]

    def body(at, beside):
        for half in range(2):
            rows = slice(half * reach, (half + 1) * reach)
            _, value, weight = heads_pair(
                q[rows, at],
                kv[rows, at],
                kv[rows, beside],
                adds[half],
                (peak[rows, at], mixed[rows, at], total[rows, at]),
            )
            windowed[rows, at] = (value / weight).astype(BF)

    pairs(width, body)
    stream = stream_in[...] + dot(windowed[...], w_out[...])
    stream_out[...] = stream
    normed[...] = rms_norm(stream).astype(BF)


def up_kernel(me, normed, w_up, *outs, chunk):
    step = outs[0].shape[1]
    for j, out in enumerate(outs):
        first = ((me[0] % PLANE) ^ j) * (CHUNKS * step) + chunk * step
        at = pl.ds(pl.multiple_of(first, step), step)
        out[...] = jax.nn.gelu(dot(normed[...], w_up[:, at])).astype(BF)


def down_kernel(me, stream, w_down, *refs):
    hidden, out = refs[:-1], refs[-1]
    step = hidden[0].shape[1]
    total = stream[...]
    for i, block in enumerate(hidden):
        chunk, j = divmod(i, PLANE)
        first = ((me[0] % PLANE) ^ j) * (CHUNKS * step) + chunk * step
        total += dot(block[...], w_down[pl.ds(pl.multiple_of(first, step), step), :])
    out[...] = total.astype(BF)


def gradient_kernel(hidden, cotangent, out):
    out[...] = dot(hidden[...], cotangent[...], ((0,), (0,))).astype(BF)


def plane_kernel(me, *refs):
    hidden, cotangent, (own, other, total) = refs[:PLANE], refs[PLANE : 2 * PLANE], refs[2 * PLANE :]
    total[...] = sum(
        dot(h[...], c[...], ((0,), (0,))) for h, c in zip(hidden, cotangent, strict=True)
    )
    rows = own.shape[0]
    for i, out in enumerate((own, other)):
        at = pl.multiple_of(((me[0] // PLANE + i) % 2) * rows, rows)
        out[...] = total[pl.ds(at, rows), :].astype(out.dtype)


def clip_kernel(me, *refs, order, unit):
    pieces, (out, sums, scaled, sent) = refs[:-4], refs[-4:]
    quarter = out.shape[0] // PLANE
    where = []
    for piece, steps in zip(pieces, order, strict=True):
        for i, (flip, base, other) in enumerate(steps):
            tile = me[0] ^ flip
            half = (tile // PLANE + other) % 2
            where.append(((tile % PLANE) * quarter + base + half * unit, piece, i))
    for at, piece, i in where:
        v = piece[i].astype(F32)
        sums[pl.ds(at // unit, 1), :] = jnp.sum(v * v, axis=0, keepdims=True)
    total = jnp.sum(jnp.sum(sums[...], axis=0, keepdims=True), axis=1, keepdims=True)
    factor = jnp.minimum(1.0, 0.5 / jnp.sqrt(total / (out.shape[0] * out.shape[1]) + 1e-06))
    copies = []
    for n, (at, piece, i) in enumerate(where):
        scaled[n] = piece[i].astype(F32) * factor
        rows = pl.ds(pl.multiple_of(at, unit), unit)
        copies.append(pltpu.make_async_copy(scaled.at[n], out.at[rows, :], sent.at[n]))
        copies[-1].start()
    for copy in copies:
        copy.wait()


def clip_whole_kernel(gradient, out):
    v = gradient[...].astype(F32)
    total = jnp.sum(jnp.sum(v * v, axis=0, keepdims=True), axis=1, keepdims=True)
    factor = jnp.minimum(1.0, 0.5 / jnp.sqrt(total / (out.shape[0] * out.shape[1]) + 1e-06))
    out[...] = v * factor


def flipped(value, k):
    return lax.ppermute(value, "tile", [(i, i ^ k) for i in range(PLANE * PLANE)])


def narrow(value):
    return value.astype(BF)


def reduced(own, other, base, hops):
    own = narrow(own + flipped(other, PLANE).astype(F32))
    own = narrow(own.astype(F32) + flipped(own, 2 * PLANE).astype(F32))
    pieces, order = [], []
    for n, (first, two) in enumerate(zip((1, 2), hops, strict=True)):
        half = flipped(own, PLANE) if n else own
        if two:
            pair = jnp.stack([half, flipped(half, first)])
            pieces += [pair, flipped(pair, 3 - first)]
            order += [[(0, base, n), (first, base, n)], [(3 - first, base, n), (3, base, n)]]
        else:
            pieces += [half[None]] + [flipped(half, j)[None] for j in range(1, PLANE)]
            order += [[(j, base, n)] for j in range(PLANE)]
    return pieces, order


def on_device(
    observations,
    instrument,
    route,
    cell_index,
    latent,
    inst_table,
    w_obs_kv,
    w_cross_q,
    w_cross_out,
    w_win_qkv,
    w_win_out,
    w_up,
    w_down,
    cotangent,
):
    tiles = lax.axis_size("tile")
    count, channels = observations.shape
    cells, width = latent.shape
    hidden_width = w_up.shape[1]
    cap = 2 * count // tiles
    split = channels // LANES
    rows = split * cap + 8
    fast = tiles == PLANE * PLANE and cap == LANES
    me = lax.axis_index("tile").reshape(1) if fast else jnp.zeros((1,), jnp.int32)
    shape = jax.ShapeDtypeStruct
    stream_shape = shape((cells, width), F32)
    half_shape = shape((cells // 2, width), BF)
    query_shape = shape((cells, width), BF)

    packed = call(
        functools.partial(pack_kernel, tiles=tiles, cap=cap),
        shape((tiles, rows, LANES), BF),
        2 * tiles * cap * count * channels,
        2 * tiles * cap * channels + 2 * count * channels,
        [FAR] * 5,
        scratch=[
            pltpu.VMEM((1, count), jnp.int32),
            pltpu.VMEM((1, count), jnp.int32),
            pltpu.VMEM((1, count), jnp.int32),
            pltpu.VMEM(inst_table.shape, BF),
            pltpu.VMEM((count, channels), BF),
            pltpu.VMEM((tiles, rows, LANES), BF),
            pltpu.SemaphoreType.DMA((5,)),
            pltpu.SemaphoreType.DMA((-(-tiles * cap // 256),)),
        ],
        out_spec=FAR,
        limit=62,
    )(
        route.reshape(1, count),
        cell_index.reshape(1, count),
        instrument.reshape(1, count),
        inst_table,
        observations,
    )

    keys = tiles * cap
    arrived = lax.all_to_all(packed, "tile", split_axis=0, concat_axis=0, tiled=True)
    if fast:
        cotangents = [flipped(cotangent, j) for j in range(1, PLANE)]
    query = call(
        query_kernel,
        query_shape,
        2 * cells * width * width,
        2 * width * width + 4 * cells * width,
        [WHOLE] * 2,
        limit=8,
    )(latent, w_cross_q)
    marks = [arrived[:, split * cap, :cap].reshape(1, keys).astype(F32)] if cap % LANES else []
    operands = (arrived, w_obs_kv, query, latent, w_cross_out, *marks)
    stream1, own, top, bottom = call(
        functools.partial(cross_kernel, cap=cap, inputs=len(operands)),
        (stream_shape, query_shape, half_shape, half_shape),
        4 * keys * channels * width + 4 * cells * keys * width,
        2 * keys * channels + 6 * width * width,
        [FAR] * len(operands),
        scratch=[pltpu.VMEM(operand.shape, operand.dtype) for operand in operands]
        + [
            pltpu.VMEM((keys, channels), BF),
            pltpu.VMEM((keys, 2 * width), BF),
            pltpu.VMEM((cells, keys), F32),
            pltpu.VMEM((cells, width), BF),
            pltpu.SemaphoreType.DMA((len(operands),)),
        ],
        transcendentals=H * cells * keys,
        limit=62,
    )(*operands)

    if not fast:
        cotangents = []
    else:
        top, bottom, *cotangents = lax.optimization_barrier((top, bottom, *cotangents))
        cotangents = [cotangent, *cotangents]
    forward = [(i, (i + 1) % tiles) for i in range(tiles)]
    backward = [(b, a) for a, b in forward]
    after = lax.ppermute(top, "tile", backward)
    before = lax.ppermute(bottom, "tile", forward)
    fetched = len(cotangents)
    partial = call(
        functools.partial(inner_kernel, fetched=fetched),
        (query_shape, stream_shape, stream_shape, stream_shape, *([query_shape] * fetched)),
        6 * cells * width * width + 4 * cells * cells * width,
        6 * width * width + 16 * cells * width,
        [WHOLE] + [FAR] * (1 + fetched),
        scratch=[
            pltpu.VMEM((cells, 2 * width), BF),
            pltpu.VMEM((cells, width), BF),
            pltpu.VMEM((cells, cells), F32),
            pltpu.SemaphoreType.DMA((1 + fetched,)),
        ],
        transcendentals=H * cells * cells,
        limit=20,
    )(w_win_qkv, own, *cotangents)
    partial, cotangents = partial[:4], partial[4:]
    stream2, normed = call(
        outer_kernel,
        (stream_shape, query_shape),
        6 * cells * width * width + 2 * cells * cells * width,
        8 * width * width + 24 * cells * width,
        [WHOLE] * 9,
        scratch=[pltpu.VMEM((cells, 2 * width), BF), pltpu.VMEM((cells, width), BF)],
        transcendentals=H * cells * cells // 2,
        limit=20,
    )(stream1, before, after, w_win_qkv, w_win_out, *partial)

    step = hidden_width // (CHUNKS * PLANE)
    hidden = [
        call(
            functools.partial(up_kernel, chunk=c),
            [shape((cells, step), BF)] * PLANE,
            2 * cells * width * hidden_width // CHUNKS,
            2 * width * hidden_width // CHUNKS + 2 * cells * hidden_width // CHUNKS,
            [SCALAR, WHOLE, WHOLE],
            transcendentals=cells * hidden_width // CHUNKS,
            limit=12,
        )(me, normed, w_up)
        for c in range(CHUNKS)
    ]
    if fast:
        received = [[h[0]] + [flipped(h[j], j) for j in range(1, PLANE)] for h in hidden]
    part = hidden_width // tiles
    if fast:
        half = shape((step // 2, width), F32)
        pieces, order = [], []
        for c in range(CHUNKS):
            own, other = call(
                plane_kernel,
                (half, shape(half.shape, BF)),
                2 * PLANE * cells * step * width,
                2 * PLANE * cells * (step + width) + 2 * step * width,
                [SCALAR] + [WHOLE] * (2 * PLANE),
                scratch=[pltpu.VMEM((step, width), F32)],
                limit=12,
            )(me, *received[c], *cotangents)
            if c == 0:
                stream2, own = lax.optimization_barrier((stream2, own))
            more, places = reduced(own, other, c * step, HOPS[c])
            pieces, order = pieces + more, order + places
        clipped = call(
            functools.partial(clip_kernel, order=order, unit=step // 2),
            shape((hidden_width, width), F32),
            4 * hidden_width * width,
            6 * hidden_width * width,
            [SCALAR] + [WHOLE] * len(pieces),
            scratch=[
                pltpu.VMEM((2 * CHUNKS * PLANE, width), F32),
                pltpu.VMEM((2 * CHUNKS * PLANE, step // 2, width), F32),
                pltpu.SemaphoreType.DMA((2 * CHUNKS * PLANE,)),
            ],
            out_spec=FAR,
            limit=24,
        )(me, *pieces)
    else:
        whole = jnp.concatenate([hidden[c][j] for j in range(PLANE) for c in range(CHUNKS)], 1)
        swapped = lax.all_to_all(
            whole.reshape(cells, tiles, part).transpose(1, 0, 2),
            "tile",
            split_axis=0,
            concat_axis=0,
            tiled=True,
        )
        gradient = call(
            gradient_kernel,
            shape((part, width), BF),
            2 * tiles * cells * part * width,
            2 * tiles * cells * (part + width),
            [WHOLE] * 2,
            limit=60,
        )(
            swapped.reshape(tiles * cells, part),
            lax.all_gather(cotangent, "tile", axis=0, tiled=True),
        )
        clipped = call(
            clip_whole_kernel,
            shape((hidden_width, width), F32),
            4 * hidden_width * width,
            6 * hidden_width * width,
            [WHOLE],
            limit=24,
        )(lax.all_gather(gradient, "tile", axis=0, tiled=True))
    latent_out = call(
        down_kernel,
        query_shape,
        2 * cells * width * hidden_width,
        2 * width * hidden_width + 2 * cells * hidden_width,
        [SCALAR] + [WHOLE] * (2 + CHUNKS * PLANE),
        limit=12,
    )(me, stream2, w_down, *[block for h in hidden for block in h])
    return (latent_out, clipped)


def solution(mesh):
    split = P(("dp", "tile"))
    rows = P(("dp", "tile"), None)
    return jax.shard_map(
        on_device,
        mesh=mesh,
        in_specs=(rows, split, rows, split, rows, P(), P(), P(), P(), P(), P(), P(), P(), rows),
        out_specs=(rows, P("dp", None)),
        check_vma=False,
    )
```
